128 devices in a mesh: frame: 16 (over z, x_lo, core), patch: 8 (over x_hi, y).
Axes of the slice: x: 4 (x_hi: 2, x_lo: 2; x = x_hi * 2 + x_lo), y: 4, z: 4, core: 2. Of those that a mesh axis runs over, the one named last changes fastest.
Arguments:
- coeffs: float32 [32, 128, 300], P('frame', 'patch'), may hold values from -4 to 4
- observed: bfloat16 [32, 128, 128, 128], P('frame', 'patch'), may hold values from -6 to 6
- object_field: float32 [128, 128, 128], P('patch', 'frame'), may hold values from -6 to 6
- mode_basis: bfloat16 [300, 128, 128], replicated, may hold values from -0.375 to 0.375
- pupil_mask: int32 [128, 128], replicated, may hold values from 0 to 1, as said below
Outputs:
- new_coeffs: float32 [32, 128, 300], P('frame', 'patch')
- new_object: float32 [128, 128, 128], P('patch', 'frame')
The draws below stay inside these ranges and needn't reach their ends.
Inputs may be any that keep to these rules, and one draw needn't show every extreme that they name: `pupil_mask`: the pupil is an annulus centred on cell 128 // 2 of each dimension with an outer radius of at least 48 cells, so it holds ones.
All inputs are finite; a program needn't handle non-finite values.
Results may differ from the reference program's by a relative error of at most 0.0035.
Values may be sent and summed in bfloat16 or wider, within the bound.
A program may use at most 128 MiB of HBM per device.

```python
import math
import jax
import jax.numpy as jnp
from jax import lax

G = 128
MODES = 300
ITERS = 2
FRAMES = 32
PATCHES = 128


def draw_pupil_mask(key, part):
    key_outer, key_inner = jax.random.split(jax.random.fold_in(key, 17))
    radius_out = jax.random.randint(key_outer, (), 3 * G // 8, G // 2 + 1)
    radius_in = jax.random.randint(key_inner, (), 0, G // 8 + 1)
    coords = jnp.arange(G, dtype=jnp.int32) - G // 2
    distance = coords[:, None] * coords[:, None] + coords[None, :] * coords[None, :]
    inside = (distance <= radius_out * radius_out) & (distance >= radius_in * radius_in)
    return jnp.where(inside, 1, 0).astype(jnp.int32)


def block_levels(rng, dims, shards, smallest, largest):
    gain = 1.0
    for axis_at, blocks in shards:
        steps = jax.random.uniform(jax.random.fold_in(jax.random.fold_in(rng, 6), axis_at), (blocks,), jnp.float32, smallest / len(shards), largest / len(shards))
        gain = gain * jnp.repeat(jnp.exp(steps), dims[axis_at] // blocks).reshape((-1,) + (1,) * (len(dims) - 1 - axis_at))
    return gain


def normal_values(stream_key, shape, scale, bound, cuts=(), held_as=jnp.bfloat16):
    entries = scale * jax.random.normal(stream_key, shape, jnp.float32)
    if cuts:
        entries = entries * block_levels(stream_key, shape, cuts, -0.22, 0.18)
    return jnp.clip(entries, -bound, bound).astype(held_as)


def setup_inputs(seed: int = 0) -> dict:
    arg_keys = jax.random.split(jax.random.key(seed), 6)
    return {
        "coeffs": normal_values(arg_keys[0], (FRAMES, PATCHES, MODES), 1.0, 4.0, ((0, 16), (1, 8)), jnp.float32),
        "observed": normal_values(arg_keys[1], (FRAMES, PATCHES, G, G), 1.0, 6.0, ((0, 16), (1, 8))),
        "object_field": normal_values(arg_keys[2], (PATCHES, G, G), 1.0, 6.0, ((0, 8), (1, 16)), jnp.float32),
        "mode_basis": normal_values(arg_keys[3], (MODES, G, G), MODES ** -0.5, 0.375),
        "pupil_mask": draw_pupil_mask(jax.random.fold_in(arg_keys[5], 71), 0),
    }


EPSILON = 1e-06
STEP_OBJECT = 0.1
STEP_COEFF = 0.2

def dft_tables(extent):
    counter = jnp.arange(extent, dtype=jnp.int32)
    product = counter[:, None] * counter[None, :] % extent
    angles = product.astype(jnp.float32) * (2.0 * math.pi / extent)
    return (jnp.cos(angles).astype(jnp.bfloat16), jnp.sin(angles).astype(jnp.bfloat16))

def right_mul(values, matrix):
    in_shape = values.shape
    result = jnp.dot(values.reshape(-1, in_shape[-1]), matrix, preferred_element_type=jnp.float32)
    return result.reshape(in_shape)

def left_mul(values, matrix):
    return jnp.einsum('jb,nbk->njk', matrix.astype(jnp.float32), values.astype(jnp.float32), precision=lax.Precision.HIGHEST)

def apply_pass(multiply, real_in, imag_in, cosine, sine_table, inverse, keep_imag):
    sign_value = 1.0 if inverse else -1.0
    real_low = real_in.astype(jnp.bfloat16)
    out_real = multiply(real_low, cosine)
    if imag_in is not None:
        imag_low = imag_in.astype(jnp.bfloat16)
        out_real = out_real - sign_value * multiply(imag_low, sine_table)
    if not keep_imag:
        return (out_real, None)
    out_imag = sign_value * multiply(real_low, sine_table)
    if imag_in is not None:
        out_imag = out_imag + multiply(imag_low, cosine)
    return (out_real, out_imag)

def transform(real_in, imag_in, cosine, sine_table, inverse, keep_imag):
    first_real, first_imag = apply_pass(right_mul, real_in, imag_in, cosine, sine_table, inverse, True)
    return apply_pass(left_mul, first_real, first_imag, cosine, sine_table, inverse, keep_imag)

def pair_terms(coeff_rows, observed_rows, spec_real, spec_imag, flat_basis, aperture, psf_scale, cosine, sine_table):
    pairs = coeff_rows.shape[0]
    extent = observed_rows.shape[-1]
    phase_map = jnp.dot(coeff_rows.astype(jnp.bfloat16), flat_basis, preferred_element_type=jnp.float32).reshape(pairs, extent, extent)
    cos_phase = jnp.cos(phase_map)
    sin_phase = jnp.sin(phase_map)
    focal_real, focal_imag = transform(aperture * cos_phase, aperture * sin_phase, cosine, sine_table, False, True)
    spread = (focal_real * focal_real + focal_imag * focal_imag) * psf_scale
    otf_real, otf_imag = transform(spread, None, cosine, sine_table, False, True)
    model_real = spec_real * otf_real - spec_imag * otf_imag
    model_imag = spec_real * otf_imag + spec_imag * otf_real
    model_image, unused = transform(model_real, model_imag, cosine, sine_table, True, False)
    residual = model_image / (extent * extent) - observed_rows.astype(jnp.float32)
    grad_real, grad_imag = transform(residual, None, cosine, sine_table, False, True)
    grad_real = grad_real / (extent * extent)
    grad_imag = grad_imag / (extent * extent)
    objg_real = grad_real * otf_real + grad_imag * otf_imag
    objg_imag = grad_imag * otf_real - grad_real * otf_imag
    half_real, half_imag = apply_pass(right_mul, objg_real, objg_imag, cosine, sine_table, True, True)
    otfg_real = grad_real * spec_real + grad_imag * spec_imag
    otfg_imag = grad_imag * spec_real - grad_real * spec_imag
    spread_grad, unused = transform(otfg_real, otfg_imag, cosine, sine_table, True, False)
    factor = 2.0 * psf_scale * spread_grad
    field_real, field_imag = transform(factor * focal_real, factor * focal_imag, cosine, sine_table, True, True)
    phase_grad = aperture * (field_imag * cos_phase - field_real * sin_phase)
    coeff_grad = lax.dot_general(phase_grad.reshape(pairs, -1).astype(jnp.bfloat16), flat_basis, (((1,), (1,)), ((), ())), preferred_element_type=jnp.float32)
    return (coeff_grad, half_real, half_imag)

def reference(coeffs, observed, object_field, mode_basis, pupil_mask):
    mode_count = mode_basis.shape[0]
    extent = mode_basis.shape[-1]
    cosine, sine_table = dft_tables(extent)
    aperture = pupil_mask.astype(jnp.float32)
    psf_scale = 1.0 / (extent * extent * jnp.sum(aperture))
    flat_basis = mode_basis.reshape(mode_count, extent * extent)
    for iteration in range(ITERS):
        rows_real, rows_imag = apply_pass(left_mul, object_field, None, cosine, sine_table, False, True)
        spec_real, spec_imag = apply_pass(right_mul, rows_real, rows_imag, cosine, sine_table, False, True)

        def frame_step(running, inputs):
            coeff_frame, observed_frame = inputs
            coeff_grad, half_real, half_imag = pair_terms(coeff_frame, observed_frame, spec_real, spec_imag, flat_basis, aperture, psf_scale, cosine, sine_table)
            object_term, unused = apply_pass(left_mul, half_real, half_imag, cosine, sine_table, True, False)
            return (running + object_term, coeff_grad)
        object_grad, coeff_grad = lax.scan(frame_step, jnp.zeros(object_field.shape, jnp.float32), (coeffs, observed))
        object_rms = jnp.sqrt(jnp.sum(object_grad * object_grad) / object_grad.size + EPSILON)
        coeff_rms = jnp.sqrt(jnp.sum(coeff_grad * coeff_grad) / coeff_grad.size + EPSILON)
        object_field = object_field - STEP_OBJECT * object_grad / object_rms
        coeffs = coeffs - STEP_COEFF * coeff_grad / coeff_rms
    return (coeffs, object_field)
```

```python
import functools
import math

import jax
import jax.numpy as jnp
import numpy as np
from jax import lax
from jax.experimental import pallas as pl
from jax.experimental.pallas import tpu as pltpu
from jax.sharding import PartitionSpec as P

ITERS = 2
EPSILON = 1e-06
STEP_OBJECT = 0.1
STEP_COEFF = 0.2
CHUNK = 8
BLK = 16
LANES = 128
MESH = pl.DeviceIdType.MESH
BF = jnp.bfloat16
F32 = jnp.float32


def fit(even):
    f = np.cos((np.arange(4000) + 0.5) * (np.pi / 8000)) * 0.5
    target = np.sqrt(2.0) * (np.cos(np.pi * f) if even else np.sin(np.pi * f) / f)
    powers = np.stack([f ** (2 * k) for k in range(6 if even else 5)], axis=1)
    coef = np.linalg.lstsq(powers, target, rcond=None)[0]
    return [float(np.float32(v)) for v in coef]


SIN_COEF = fit(False)
COS_COEF = fit(True)


def horner(z, coef):
    acc = coef[-1] * z + coef[-2]
    for value in coef[-3::-1]:
        acc = acc * z + value
    return acc


def sincos(x):
    turns = x * (1.0 / (2.0 * math.pi))
    f = turns - jnp.round(turns)
    z = f * f
    s = f * horner(z, SIN_COEF)
    c = horner(z, COS_COEF)
    return s * c, 1.0 - s * s


def dot(a, b):
    return jnp.dot(a, b, preferred_element_type=F32)


def swap_blocks(m):
    n = LANES
    return jnp.concatenate(
        [
            jnp.concatenate([m[:n, :n], m[n:, :n]], axis=1),
            jnp.concatenate([m[:n, n:], m[n:, n:]], axis=1),
        ],
        axis=0,
    )


def stack(m):
    return jnp.concatenate([m[:, :LANES], m[:, LANES:]], axis=0)


def tables(extent):
    counter = np.arange(extent)
    angles = (counter[:, None] * counter[None, :] % extent).astype(np.float32) * np.float32(
        2.0 * math.pi / extent
    )
    c, s = np.cos(angles), np.sin(angles)
    fwd = np.block([[c, -s], [s, c]]).astype(np.float32)
    inv = np.block([[c, s], [-s, c]]).astype(np.float32)
    return jnp.asarray(fwd, F32).astype(BF), jnp.asarray(inv, F32).astype(BF)


def patch_steps(phases, mask, spec, observed, scale, tabs, emit):
    t1, t2, t1s, t2s = tabs
    g = LANES
    trig = [sincos(p) for p in phases]
    cos = jnp.concatenate([c * mask for s, c in trig], axis=1)
    sin = jnp.concatenate([s * mask for s, c in trig], axis=1)
    x = swap_blocks(jnp.concatenate([cos.astype(BF), sin.astype(BF)], axis=0))
    y = dot(x, t1)
    yield
    focal = dot(t2, swap_blocks(y.astype(BF)))
    yield
    fr, fi = focal[:g], focal[g:]
    spread = (fr * fr + fi * fi) * scale
    y = dot(stack(spread.astype(BF)), t1[:g])
    yield
    otf = dot(t2, swap_blocks(y.astype(BF)))
    yield
    otr, oti = otf[:g], otf[g:]
    sr = jnp.concatenate([spec[:, :g]] * 2, axis=1)
    si = jnp.concatenate([spec[:, g:]] * 2, axis=1)
    mr = (sr * otr - si * oti).astype(BF)
    mi = (sr * oti + si * otr).astype(BF)
    y = dot(swap_blocks(jnp.concatenate([mr, mi], axis=0)), t2)
    yield
    image = dot(t1s[:g], swap_blocks(y.astype(BF)))
    yield
    obs = jnp.concatenate([o.astype(F32) for o in observed], axis=1)
    residual = image - obs
    y = dot(stack(residual.astype(BF)), t1[:g])
    yield
    grad = dot(t2s, swap_blocks(y.astype(BF)))
    yield
    gr, gi = grad[:g], grad[g:]
    ar = (gr * otr + gi * oti).astype(BF)
    ai = (gi * otr - gr * oti).astype(BF)
    half = dot(swap_blocks(jnp.concatenate([ar, ai], axis=0)), t2)
    br = (gr * sr + gi * si).astype(BF)
    bi = (gi * sr - gr * si).astype(BF)
    y = dot(swap_blocks(jnp.concatenate([br, bi], axis=0)), t2)
    yield
    term = dot(t1[:g], stack((half[:g] + half[g:]).astype(BF)))
    spread_grad = dot(t1[:g], swap_blocks(y.astype(BF)))
    yield
    factor = (2.0 * scale) * spread_grad
    fr, fi = (factor * fr).astype(BF), (factor * fi).astype(BF)
    y = dot(swap_blocks(jnp.concatenate([fr, fi], axis=0)), t2)
    yield
    field = dot(t1, swap_blocks(y.astype(BF)))
    yield
    emit(term, (field[g:] * cos - field[:g] * sin).astype(BF))


def interleave(work, lag):
    waiting, running, tick = list(work), [], 0
    while waiting or running:
        if waiting and tick % lag == 0:
            running.append(waiting.pop(0))
        running = [w for w in running if next(w, "done") is None]
        tick += 1


def kernel(
    sizes,
    coeff_in,
    object_in,
    mask_in,
    fwd_in,
    inv_in,
    expand_in,
    fold_in,
    observed_hbm,
    basis_hbm,
    coeff_out,
    object_out,
    basis,
    observed,
    spread_rows,
    phase,
    spectrum,
    slopes,
    wide,
    ag_send,
    ag_recv,
    rs_send,
    rs_recv,
    sc_send,
    sc_mid,
    sc_recv_frame,
    sc_recv_patch,
    load_sem,
    ag_sem,
    rs_sem,
    sc_sem,
):
    frames, patches, modes, n_frame, n_patch, rows = sizes
    g = LANES
    pairs = frames * patches
    groups = -(-modes // BLK)
    blocks = g // BLK
    me = lax.axis_index("frame")
    my_patch = lax.axis_index("patch")

    load_basis = pltpu.make_async_copy(basis_hbm, basis.at[pl.ds(0, modes)], load_sem.at[0])
    load_observed = pltpu.make_async_copy(observed_hbm, observed, load_sem.at[1])
    load_basis.start()
    load_observed.start()

    barrier = pltpu.get_barrier_semaphore()
    for k in range(1, n_frame):
        peer = lax.rem(me + k, n_frame)
        pl.semaphore_signal(barrier, inc=1, device_id={"frame": peer}, device_id_type=MESH)
    for k in range(1, n_patch):
        peer = lax.rem(my_patch + k, n_patch)
        pl.semaphore_signal(barrier, inc=1, device_id={"patch": peer}, device_id_type=MESH)

    object_out[...] = object_in[...]
    coeff_out[...] = coeff_in[...]
    ag_send[...] = object_in[...].astype(BF)
    if groups * BLK > modes:
        basis[pl.ds(modes, groups * BLK - modes)] = jnp.zeros((groups * BLK - modes, g, g), BF)
    mask = mask_in[...].astype(F32)
    scale = 1.0 / (g * g * jnp.sum(mask))
    sc_send[...] = jnp.zeros(sc_send.shape, F32)
    pl.semaphore_wait(barrier, n_frame + n_patch - 2)

    def gather(start):
        for k in range(1, n_frame):
            copy = pltpu.make_async_remote_copy(
                src_ref=ag_send,
                dst_ref=ag_recv.at[me],
                send_sem=ag_sem.at[0],
                recv_sem=ag_sem.at[1],
                device_id={"frame": lax.rem(me + k, n_frame)},
                device_id_type=MESH,
            )
            copy.start()

    def all_of(buffer, out, sem, axis, count):
        return pltpu.make_async_remote_copy(
            src_ref=out.at[pl.ds(0, count)],
            dst_ref=buffer.at[pl.ds(0, count)],
            send_sem=sem.at[0],
            recv_sem=sem.at[1],
            device_id={axis: 0},
            device_id_type=MESH,
        )

    row_of = lax.rem(lax.broadcasted_iota(jnp.int32, (BLK, 2 * g), 0), BLK)
    lane_of = lax.rem(lax.broadcasted_iota(jnp.int32, (BLK, 2 * g), 1), BLK)
    diagonal = row_of == lane_of

    def phase_maps():
        wide[...] = dot(coeff_out[...].astype(BF), expand_in[...])

        def spread_group(at, carry):
            values = wide[pl.ds(pl.multiple_of(at * pairs, pairs), pairs), :]
            values = jnp.broadcast_to(values[:, None, :], (pairs, BLK, 2 * g))
            values = jnp.where(diagonal[None], values, 0.0).astype(BF)
            spread_rows[at] = values.reshape(pairs * BLK, 2 * g)
            return carry

        lax.fori_loop(0, groups, spread_group, 0)

    def phase_products():
        lhs = jnp.concatenate([spread_rows[k] for k in range(groups)], axis=1)

        def block(at, carry):
            first = pl.multiple_of(at * 2 * BLK, 2 * BLK)
            depth = groups * BLK * BLK
            rhs = jnp.concatenate(
                [
                    basis[:, pl.ds(first, BLK), :].reshape(depth, g),
                    basis[:, pl.ds(first + BLK, BLK), :].reshape(depth, g),
                ],
                axis=1,
            )
            out = dot(lhs, rhs)
            phase[:, pl.ds(first, BLK), :] = out[:, :g].reshape(pairs, BLK, g)
            phase[:, pl.ds(first + BLK, BLK), :] = out[:, g:].reshape(pairs, BLK, g)
            return carry

        lax.fori_loop(0, blocks // 2, block, 0)

    def spectra():
        for q in range(0, patches, 2):
            pieces = [
                ag_recv[:, q + u].astype(F32).reshape(g, g).astype(BF) for u in range(2)
            ]
            left = dot(inv_in[:, :g], jnp.concatenate(pieces, axis=1))
            out = dot(swap_blocks(left.astype(BF)), fwd_in[...])
            spectrum[q] = out[:g]
            spectrum[q + 1] = out[g:]

    inverse = 1.0 / (g * g)

    def patch_chunk(at, carry):
        fwd, inv = fwd_in[...], inv_in[...]
        tabs = (fwd, inv, fwd * BF(inverse), inv * BF(inverse))

        def one(q):
            def emit(term, slope):
                rs_send[:, q] = term.reshape(n_frame, rows, g).astype(BF)
                for f in range(frames):
                    for b in range(blocks):
                        slopes[f * patches + q, :, pl.ds(b * g, g)] = slope[
                            b * BLK : (b + 1) * BLK, f * g : (f + 1) * g
                        ]

            picks = [f * patches + q for f in range(frames)]
            return patch_steps(
                [phase[p] for p in picks],
                mask,
                spectrum[q],
                [observed[p] for p in picks],
                scale,
                tabs,
                emit,
            )

        interleave([one(at * CHUNK + u) for u in range(CHUNK)], 1)
        for k in range(1, n_frame):
            peer = lax.rem(me + k, n_frame)
            part = pl.ds(pl.multiple_of(at * CHUNK, CHUNK), CHUNK)
            copy = pltpu.make_async_remote_copy(
                src_ref=rs_send.at[peer, part],
                dst_ref=rs_recv.at[me, part],
                send_sem=rs_sem.at[0],
                recv_sem=rs_sem.at[1],
                device_id={"frame": peer},
                device_id_type=MESH,
            )
            copy.start()
        return carry

    def coeff_products():
        lhs = slopes[...].reshape(pairs * BLK, blocks * g)

        def group(at, carry):
            first = pl.multiple_of(at * BLK, BLK)
            rhs = jnp.concatenate(
                [
                    basis[pl.ds(first, BLK), b * BLK : (b + 1) * BLK, :].reshape(BLK * BLK, g)
                    for b in range(blocks)
                ],
                axis=1,
            )
            out = lax.dot_general(lhs, rhs, (((1,), (1,)), ((), ())), preferred_element_type=F32)
            out = out.reshape(pairs, BLK, BLK * BLK)
            out = jnp.where(diagonal[None], out, 0.0)
            wide[pl.ds(pl.multiple_of(at * pairs, pairs), pairs), :] = jnp.sum(out, axis=1)
            return carry

        lax.fori_loop(0, groups, group, 0)
        rest, total = wide[...], 0.0
        for part in range(3):
            low = rest.astype(BF)
            total = total + dot(low, fold_in[...])
            rest = rest - low.astype(F32)
        return total

    def exchange(axis, count, own, send, recv, sem):
        for k in range(1, count):
            copy = pltpu.make_async_remote_copy(
                src_ref=send,
                dst_ref=recv.at[own],
                send_sem=sem.at[0],
                recv_sem=sem.at[1],
                device_id={axis: lax.rem(own + k, count)},
                device_id_type=MESH,
            )
            copy.start()

    for iteration in range(ITERS):
        gather(iteration)
        ag_recv[me] = ag_send[...]
        phase_maps()
        if iteration == 0:
            load_basis.wait()
        phase_products()
        both = all_of(ag_recv, ag_recv, ag_sem, "frame", n_frame - 1)
        both.wait_recv()
        both.wait_send()
        spectra()
        if iteration == 0:
            load_observed.wait()
        lax.fori_loop(0, patches // CHUNK, patch_chunk, 0)
        coeff_grad = coeff_products()
        both = all_of(rs_recv, rs_send, rs_sem, "frame", n_frame - 1)
        both.wait_recv()
        own_grad = rs_send[me].astype(F32)
        for k in range(1, n_frame):
            own_grad = own_grad + rs_recv[lax.rem(me + k, n_frame)].astype(F32)
        both.wait_send()

        sc_send[0:1, :] = jnp.sum(jnp.sum(own_grad * own_grad, axis=0), axis=0, keepdims=True)
        sc_send[1:2, 0:BLK] = jnp.sum(coeff_grad * coeff_grad, axis=0, keepdims=True)
        exchange("frame", n_frame, me, sc_send, sc_recv_frame, sc_sem.at[0])
        both = all_of(sc_recv_frame, sc_recv_frame, sc_sem.at[0], "frame", n_frame - 1)
        both.wait_recv()
        both.wait_send()
        total = sc_send[...]
        for k in range(1, n_frame):
            total = total + sc_recv_frame[lax.rem(me + k, n_frame)]
        sc_mid[...] = total
        from_patch = sc_recv_patch.at[iteration]
        exchange("patch", n_patch, my_patch, sc_mid, from_patch, sc_sem.at[1 + iteration])
        both = all_of(from_patch, from_patch, sc_sem.at[1 + iteration], "patch", n_patch - 1)
        both.wait_recv()
        both.wait_send()
        for k in range(1, n_patch):
            total = total + from_patch[lax.rem(my_patch + k, n_patch)]
        object_count = patches * rows * g * n_frame * n_patch
        coeff_count = pairs * modes * n_frame * n_patch
        object_rms = jnp.sqrt(jnp.sum(total[0:1], keepdims=True) / object_count + EPSILON)
        coeff_rms = jnp.sqrt(jnp.sum(total[1:2], keepdims=True) / coeff_count + EPSILON)
        coeff_out[...] = coeff_out[...] - STEP_COEFF * coeff_grad / coeff_rms
        updated = object_out[...] - STEP_OBJECT * own_grad / object_rms[None]
        object_out[...] = updated
        if iteration + 1 < ITERS:
            ag_send[...] = updated.astype(BF)


def local(n_frame, n_patch, coeffs, observed, object_field, mode_basis, pupil_mask):
    frames, patches, modes = coeffs.shape
    rows, g = object_field.shape[1:]
    pairs = frames * patches
    groups = -(-modes // BLK)
    padded = groups * BLK
    wide_in = jnp.pad(coeffs.reshape(pairs, modes), ((0, 0), (0, padded - modes)))
    wide_in = wide_in.reshape(pairs, groups, BLK).transpose(1, 0, 2).reshape(groups * pairs, BLK)
    fwd, inv = tables(g)
    expand = np.kron(np.eye(BLK), np.ones((1, BLK)))
    vmem = pl.BlockSpec(memory_space=pltpu.VMEM)
    hbm = pl.BlockSpec(memory_space=pl.ANY)
    dma = pltpu.SemaphoreType.DMA
    sizes = (frames, patches, modes, n_frame, n_patch, rows)
    new_coeffs, new_object = pl.pallas_call(
        functools.partial(kernel, sizes),
        out_shape=[
            jax.ShapeDtypeStruct((groups * pairs, BLK), F32),
            jax.ShapeDtypeStruct(object_field.shape, F32),
        ],
        in_specs=[vmem] * 7 + [hbm] * 2,
        out_specs=[vmem, vmem],
        scratch_shapes=[
            pltpu.VMEM((padded, g, g), BF),
            pltpu.VMEM((pairs, g, g), BF),
            pltpu.VMEM((groups, pairs * BLK, 2 * g), BF),
            pltpu.VMEM((pairs, g, g), F32),
            pltpu.VMEM((patches, g, 2 * g), F32),
            pltpu.VMEM((pairs, BLK, g * g // BLK), BF),
            pltpu.VMEM((groups * pairs, 2 * g), F32),
            pltpu.VMEM((patches, rows, g), BF),
            pltpu.VMEM((n_frame, patches, rows, g), BF),
            pltpu.VMEM((n_frame, patches, rows, g), BF),
            pltpu.VMEM((n_frame, patches, rows, g), BF),
            pltpu.VMEM((8, g), F32),
            pltpu.VMEM((8, g), F32),
            pltpu.VMEM((n_frame, 8, g), F32),
            pltpu.VMEM((ITERS, n_patch, 8, g), F32),
            dma((2,)),
            dma((2,)),
            dma((2,)),
            dma((1 + ITERS, 2)),
        ],
        compiler_params=pltpu.CompilerParams(
            collective_id=0, has_side_effects=True, vmem_limit_bytes=62 * 1024 * 1024
        ),
    )(
        wide_in,
        object_field,
        pupil_mask,
        fwd,
        inv,
        jnp.asarray(expand, BF),
        jnp.asarray(expand.T, BF),
        observed.reshape(pairs, g, g),
        mode_basis,
    )
    new_coeffs = new_coeffs.reshape(groups, pairs, BLK).transpose(1, 0, 2).reshape(pairs, padded)
    return new_coeffs[:, :modes].reshape(coeffs.shape), new_object


def solution(mesh):
    in_specs = (
        P("frame", "patch", None),
        P("frame", "patch", None, None),
        P("patch", "frame", None),
        P(),
        P(),
    )
    out_specs = (P("frame", "patch", None), P("patch", "frame", None))
    run = functools.partial(local, mesh.shape["frame"], mesh.shape["patch"])
    return jax.shard_map(run, mesh=mesh, in_specs=in_specs, out_specs=out_specs, check_vma=False)
```

```python
import functools
import math

import jax
import jax.numpy as jnp
import numpy as np
from jax import lax
from jax.experimental import pallas as pl
from jax.experimental.pallas import tpu as pltpu
from jax.sharding import PartitionSpec as P

EPSILON = 1e-06
STEP_OBJECT = 0.1
STEP_COEFF = 0.2
CHUNK = 8
BLK = 8
PARTS = 10
LANES = 128
MESH = pl.DeviceIdType.MESH
BF = jnp.bfloat16
F32 = jnp.float32


def fit(even):
    f = np.cos((np.arange(4000) + 0.5) * (np.pi / 8000)) * 0.5
    target = np.sqrt(2.0) * (np.cos(np.pi * f) if even else np.sin(np.pi * f) / f)
    powers = np.stack([f ** (2 * k) for k in range(6 if even else 5)], axis=1)
    coef = np.linalg.lstsq(powers, target, rcond=None)[0]
    return [float(np.float32(v)) for v in coef]


SIN_COEF = fit(False)
COS_COEF = fit(True)


def horner(z, coef):
    acc = coef[-1] * z + coef[-2]
    for value in coef[-3::-1]:
        acc = acc * z + value
    return acc


def sincos(x):
    turns = x * (1.0 / (2.0 * math.pi))
    f = turns - jnp.round(turns)
    z = f * f
    s = f * horner(z, SIN_COEF)
    c = horner(z, COS_COEF)
    return s * c, 1.0 - s * s


def dot(a, b):
    return jnp.dot(a, b, preferred_element_type=F32)


def swap_blocks(m):
    n = LANES
    return jnp.concatenate(
        [
            jnp.concatenate([m[:n, :n], m[n:, :n]], axis=1),
            jnp.concatenate([m[:n, n:], m[n:, n:]], axis=1),
        ],
        axis=0,
    )


def stack(m):
    return jnp.concatenate([m[:, :LANES], m[:, LANES:]], axis=0)


def tables(extent):
    counter = np.arange(extent)
    angles = (counter[:, None] * counter[None, :] % extent).astype(np.float32) * np.float32(
        2.0 * math.pi / extent
    )
    c, s = np.cos(angles), np.sin(angles)
    fwd = np.block([[c, -s], [s, c]]).astype(np.float32)
    inv = np.block([[c, s], [-s, c]]).astype(np.float32)
    return jnp.asarray(fwd, F32).astype(BF), jnp.asarray(inv, F32).astype(BF)


def patch_steps(phases, mask, spec, observed, scale, tabs, emit):
    t1, t2, t1s, t2s = tabs
    g = LANES
    trig = [sincos(p) for p in phases]
    cos = jnp.concatenate([c * mask for s, c in trig], axis=1)
    sin = jnp.concatenate([s * mask for s, c in trig], axis=1)
    x = swap_blocks(jnp.concatenate([cos.astype(BF), sin.astype(BF)], axis=0))
    y = dot(x, t1)
    yield
    focal = dot(t2, swap_blocks(y.astype(BF)))
    yield
    fr, fi = focal[:g], focal[g:]
    spread = (fr * fr + fi * fi) * scale
    y = dot(stack(spread.astype(BF)), t1[:g])
    yield
    otf = dot(t2, swap_blocks(y.astype(BF)))
    yield
    otr, oti = otf[:g], otf[g:]
    sr = jnp.concatenate([spec[:, :g]] * 2, axis=1)
    si = jnp.concatenate([spec[:, g:]] * 2, axis=1)
    mr = (sr * otr - si * oti).astype(BF)
    mi = (sr * oti + si * otr).astype(BF)
    y = dot(swap_blocks(jnp.concatenate([mr, mi], axis=0)), t2)
    yield
    image = dot(t1s[:g], swap_blocks(y.astype(BF)))
    yield
    obs = jnp.concatenate([o.astype(F32) for o in observed], axis=1)
    residual = image - obs
    y = dot(stack(residual.astype(BF)), t1[:g])
    yield
    grad = dot(t2s, swap_blocks(y.astype(BF)))
    yield
    gr, gi = grad[:g], grad[g:]
    ar = (gr * otr + gi * oti).astype(BF)
    ai = (gi * otr - gr * oti).astype(BF)
    half = dot(swap_blocks(jnp.concatenate([ar, ai], axis=0)), t2)
    br = (gr * sr + gi * si).astype(BF)
    bi = (gi * sr - gr * si).astype(BF)
    y = dot(swap_blocks(jnp.concatenate([br, bi], axis=0)), t2)
    yield
    term = dot(t1[:g], stack((half[:g] + half[g:]).astype(BF)))
    spread_grad = dot(t1[:g], swap_blocks(y.astype(BF)))
    yield
    factor = (2.0 * scale) * spread_grad
    fr, fi = (factor * fr).astype(BF), (factor * fi).astype(BF)
    y = dot(swap_blocks(jnp.concatenate([fr, fi], axis=0)), t2)
    yield
    field = dot(t1, swap_blocks(y.astype(BF)))
    yield
    emit(term, field[g:] * cos - field[:g] * sin)


def interleave(work, lag):
    waiting, running, tick = list(work), [], 0
    while waiting or running:
        if waiting and tick % lag == 0:
            running.append(waiting.pop(0))
        running = [w for w in running if next(w, "done") is None]
        tick += 1


def kernel(
    sizes,
    coeff_in,
    object_in,
    mask_in,
    fwd_in,
    inv_in,
    expand_in,
    fold_in,
    observed_hbm,
    basis_hbm,
    coeff_out,
    object_out,
    staged,
    basis,
    observed,
    rows_left,
    phase,
    phase_step,
    spectrum,
    slopes,
    wide,
    coeff_now,
    turned,
    kept,
    ag_send,
    ag_recv,
    rs_send,
    rs_recv,
    sc_send,
    sc_mid,
    sc_frame,
    sc_patch,
    basis_sem,
    load_sem,
    ag_sem,
    rs_sem,
    sc_sem,
):
    frames, patches, modes, n_frame, n_patch, rows = sizes
    g = LANES
    pairs = frames * patches
    blocks = g // BLK
    depth = modes * BLK
    span = 2 * g
    groups = -(-depth // span)
    lane_blocks = -(-modes // g)
    part = modes // PARTS
    me = lax.axis_index("frame")
    my_patch = lax.axis_index("patch")

    loads = [
        pltpu.make_async_copy(
            basis_hbm.at[pl.ds(k * part, part)], staged.at[pl.ds(k * part, part)], basis_sem.at[k]
        )
        for k in range(PARTS)
    ]
    for load in loads:
        load.start()
    load_observed = pltpu.make_async_copy(observed_hbm, observed, load_sem)
    load_observed.start()

    barrier = pltpu.get_barrier_semaphore()
    for k in range(1, n_frame):
        peer = lax.rem(me + k, n_frame)
        pl.semaphore_signal(barrier, inc=1, device_id={"frame": peer}, device_id_type=MESH)
    for k in range(1, n_patch):
        peer = lax.rem(my_patch + k, n_patch)
        pl.semaphore_signal(barrier, inc=1, device_id={"patch": peer}, device_id_type=MESH)

    ag_send[0] = object_in[...].astype(BF)
    coeff_now[...] = jnp.zeros(coeff_now.shape, F32)
    coeff_now[:, 0:modes] = coeff_in[...]
    wide[...] = jnp.zeros(wide.shape, F32)
    basis[:, pl.ds(depth, groups * span - depth), :] = jnp.zeros(
        (blocks, groups * span - depth, g), BF
    )
    mask = mask_in[...].astype(F32)
    scale = 1.0 / (g * g * jnp.sum(mask))
    sc_send[...] = jnp.zeros(sc_send.shape, F32)

    def gather(at):
        for k in range(1, n_frame):
            copy = pltpu.make_async_remote_copy(
                src_ref=ag_send.at[at],
                dst_ref=ag_recv.at[at, me],
                send_sem=ag_sem.at[at, 0],
                recv_sem=ag_sem.at[at, 1],
                device_id={"frame": lax.rem(me + k, n_frame)},
                device_id_type=MESH,
            )
            copy.start()

    def all_of(buffer, out, sem, axis, count):
        return pltpu.make_async_remote_copy(
            src_ref=out.at[pl.ds(0, count)],
            dst_ref=buffer.at[pl.ds(0, count)],
            send_sem=sem.at[0],
            recv_sem=sem.at[1],
            device_id={axis: 0},
            device_id_type=MESH,
        )

    row_of = lax.broadcasted_iota(jnp.int32, (BLK, span), 0)
    lane_of = lax.rem(lax.broadcasted_iota(jnp.int32, (BLK, span), 1), BLK)
    diagonal = row_of == lane_of

    def left_rows(pieces):
        for k in range(lane_blocks):
            width = min(groups * span - k * g * BLK, g * BLK)
            values = dot(pieces[k].astype(BF), expand_in[:, :width])
            for b in range(width // span):
                cut = values[:, b * span : (b + 1) * span]
                cut = jnp.broadcast_to(cut[:, None, :], (pairs, BLK, span))
                cut = jnp.where(diagonal[None], cut, 0.0)
                first = k * g * BLK + b * span
                rows_left[:, first : first + span] = cut.reshape(pairs * BLK, span).astype(BF)

    def basis_products(out_ref, start, stop):
        lhs = rows_left[:, :depth]

        def block(at, carry):
            rhs = jnp.concatenate([basis[2 * at, :depth, :], basis[2 * at + 1, :depth, :]], axis=1)
            out = dot(lhs, rhs)
            first = pl.multiple_of(at * 2 * BLK, 2 * BLK)
            out_ref[:, pl.ds(first, BLK), :] = out[:, :g].reshape(pairs, BLK, g)
            out_ref[:, pl.ds(first + BLK, BLK), :] = out[:, g:].reshape(pairs, BLK, g)
            return carry

        lax.fori_loop(start, stop, block, 0, unroll=2)

    def relay(k):
        def block(b, carry):
            taken = staged[pl.ds(k * part, part), pl.ds(pl.multiple_of(b * 2 * BLK, 2 * BLK), 2 * BLK), :]
            taken = taken.astype(F32)
            for h in range(2):
                half = taken[:, h * BLK : (h + 1) * BLK].reshape(part * BLK, g)
                basis[2 * b + h, pl.ds(k * part * BLK, part * BLK), :] = half.astype(BF)
            return carry

        lax.fori_loop(0, blocks // 2, block, 0)

    def spectra(rows_of):
        for q in range(0, patches, 2):
            pieces = [rows_of(q + u).reshape(g, g).astype(BF) for u in range(2)]
            left = dot(inv_in[:, :g], jnp.concatenate(pieces, axis=1))
            out = dot(swap_blocks(left.astype(BF)), fwd_in[...])
            spectrum[q] = out[:g]
            spectrum[q + 1] = out[g:]

    inverse = 1.0 / (g * g)

    def patch_chunk(phase_of, at, carry):
        fwd, inv = fwd_in[...], inv_in[...]
        tabs = (fwd, inv, fwd * BF(inverse), inv * BF(inverse))

        def one(q):
            def emit(term, slope):
                rs_send[:, q] = term.reshape(n_frame, rows, g).astype(BF)
                first = pl.multiple_of(q * frames * BLK, frames * BLK)
                for b in range(blocks):
                    cut = slope[b * BLK : (b + 1) * BLK]
                    cut = jnp.concatenate([cut[:, f * g : (f + 1) * g] for f in range(frames)], axis=0)
                    slopes[pl.ds(first, frames * BLK), b * g : (b + 1) * g] = cut.astype(BF)

            picks = [f * patches + q for f in range(frames)]
            return patch_steps(
                [phase_of(p) for p in picks],
                mask,
                spectrum[q],
                [observed[p] for p in picks],
                scale,
                tabs,
                emit,
            )

        interleave([one(at * CHUNK + u) for u in range(CHUNK)], 1)
        for k in range(1, n_frame):
            peer = lax.rem(me + k, n_frame)
            some = pl.ds(pl.multiple_of(at * CHUNK, CHUNK), CHUNK)
            copy = pltpu.make_async_remote_copy(
                src_ref=rs_send.at[peer, some],
                dst_ref=rs_recv.at[me, some],
                send_sem=rs_sem.at[0],
                recv_sem=rs_sem.at[1],
                device_id={"frame": peer},
                device_id_type=MESH,
            )
            copy.start()
        return carry

    def coeff_products():
        lhs = slopes[...]

        def group(at, carry):
            first = pl.multiple_of(at * span, span)
            rhs = jnp.concatenate([basis[b, pl.ds(first, span), :] for b in range(blocks)], axis=1)
            out = lax.dot_general(lhs, rhs, (((1,), (1,)), ((), ())), preferred_element_type=F32)
            out = jnp.where(diagonal[None], out.reshape(pairs, BLK, span), 0.0)
            wide[at] = jnp.sum(out, axis=1)
            return carry

        lax.fori_loop(0, groups, group, 0, unroll=2)
        per = g * BLK // span
        rest = jnp.concatenate(
            [
                jnp.concatenate([wide[k * per + b] for b in range(per)], axis=1)
                for k in range(lane_blocks)
            ],
            axis=0,
        )
        total = 0.0
        for _ in range(3):
            low = rest.astype(BF)
            total = total + dot(low, fold_in[...])
            rest = rest - low.astype(F32)
        pieces = []
        for k in range(lane_blocks):
            turned[k] = total[k * pairs : (k + 1) * pairs]
            pieces.append(
                jnp.concatenate(
                    [turned[k, pl.ds(f, patches, stride=frames), :] for f in range(frames)], axis=0
                )
            )
        return pieces

    def exchange(axis, count, own, send, recv, sem):
        for k in range(1, count):
            copy = pltpu.make_async_remote_copy(
                src_ref=send,
                dst_ref=recv.at[own],
                send_sem=sem.at[0],
                recv_sem=sem.at[1],
                device_id={axis: lax.rem(own + k, count)},
                device_id_type=MESH,
            )
            copy.start()

    def frame_sum():
        both = all_of(sc_frame, sc_frame, sc_sem.at[0], "frame", n_frame - 1)
        both.wait_recv()
        both.wait_send()
        total = sc_send[...]
        for k in range(1, n_frame):
            total = total + sc_frame[lax.rem(me + k, n_frame)]
        sc_mid[...] = total

    def patch_sum(at):
        recv, sem = sc_patch.at[at], sc_sem.at[1 + at]
        both = all_of(recv, recv, sem, "patch", n_patch - 1)
        both.wait_recv()
        both.wait_send()
        total = sc_mid[...]
        for k in range(1, n_patch):
            total = total + recv[lax.rem(my_patch + k, n_patch)]
        object_count = patches * rows * g * n_frame * n_patch
        coeff_count = pairs * modes * n_frame * n_patch
        object_rms = jnp.sqrt(jnp.sum(total[0:1], keepdims=True) / object_count + EPSILON)
        coeff_rms = jnp.sqrt(jnp.sum(total[1:2], keepdims=True) / coeff_count + EPSILON)
        return STEP_OBJECT / object_rms, STEP_COEFF / coeff_rms

    def finish_iteration():
        pieces = coeff_products()
        both = all_of(rs_recv, rs_send, rs_sem, "frame", n_frame - 1)
        both.wait_recv()
        own = rs_send[me].astype(F32)
        for k in range(1, n_frame):
            own = own + rs_recv[lax.rem(me + k, n_frame)].astype(F32)
        both.wait_send()
        sc_send[0:1, :] = jnp.sum(jnp.sum(own * own, axis=0), axis=0, keepdims=True)
        squares = sum(piece * piece for piece in pieces)
        sc_send[1:2, :] = jnp.sum(squares, axis=0, keepdims=True)
        return pieces, own

    halfway = blocks // 4

    left_rows([coeff_now[:, k * g : (k + 1) * g] for k in range(lane_blocks)])
    pl.semaphore_wait(barrier, n_frame + n_patch - 2)
    gather(0)
    ag_recv[0, me] = ag_send[0]
    for k in range(PARTS):
        loads[k].wait()
        relay(k)
    basis_products(phase, 0, blocks // 2)
    both = all_of(ag_recv.at[0], ag_recv.at[0], ag_sem.at[0], "frame", n_frame - 1)
    both.wait_recv()
    both.wait_send()
    spectra(lambda q: ag_recv[0, :, q].astype(F32))
    load_observed.wait()
    lax.fori_loop(0, patches // CHUNK, functools.partial(patch_chunk, lambda p: phase[p]), 0)
    pieces, own = finish_iteration()
    ag_send[1] = own.astype(BF)
    exchange("frame", n_frame, me, sc_send, sc_frame, sc_sem.at[0])

    left_rows(pieces)
    gather(1)
    ag_recv[1, me] = ag_send[1]
    for k in range(lane_blocks):
        kept[k] = pieces[k]
    object_out[...] = own
    basis_products(phase_step, 0, halfway)
    frame_sum()
    exchange("patch", n_patch, my_patch, sc_mid, sc_patch.at[0], sc_sem.at[1])
    basis_products(phase_step, halfway, blocks // 2)
    object_step, coeff_step = patch_sum(0)
    object_out[...] = object_in[...] - object_step[None] * object_out[...]
    for k in range(lane_blocks):
        cut = slice(k * g, (k + 1) * g)
        coeff_now[:, cut] = coeff_now[:, cut] - coeff_step * kept[k]
    both = all_of(ag_recv.at[1], ag_recv.at[1], ag_sem.at[1], "frame", n_frame - 1)
    both.wait_recv()
    both.wait_send()

    spectra(
        lambda q: ag_recv[0, :, q].astype(F32) - object_step[None] * ag_recv[1, :, q].astype(F32)
    )
    lax.fori_loop(
        0,
        patches // CHUNK,
        functools.partial(patch_chunk, lambda p: phase[p] - coeff_step * phase_step[p]),
        0,
    )
    pieces, own = finish_iteration()
    exchange("frame", n_frame, me, sc_send, sc_frame, sc_sem.at[0])
    frame_sum()
    exchange("patch", n_patch, my_patch, sc_mid, sc_patch.at[1], sc_sem.at[2])
    object_step, coeff_step = patch_sum(1)
    object_out[...] = object_out[...] - object_step[None] * own
    for k in range(lane_blocks):
        width = min(g, modes - k * g)
        cut = slice(k * g, k * g + width)
        coeff_out[:, cut] = coeff_now[:, cut] - coeff_step * pieces[k][:, :width]


def local(n_frame, n_patch, coeffs, observed, object_field, mode_basis, pupil_mask):
    frames, patches, modes = coeffs.shape
    rows, g = object_field.shape[1:]
    pairs = frames * patches
    blocks = g // BLK
    span = 2 * g
    padded = -(-modes * BLK // span) * span
    lane_blocks = -(-modes // g)
    fwd, inv = tables(g)
    expand = np.kron(np.eye(g), np.ones((1, BLK)))
    vmem = pl.BlockSpec(memory_space=pltpu.VMEM)
    hbm = pl.BlockSpec(memory_space=pl.ANY)
    dma = pltpu.SemaphoreType.DMA
    sizes = (frames, patches, modes, n_frame, n_patch, rows)
    new_coeffs, new_object = pl.pallas_call(
        functools.partial(kernel, sizes),
        out_shape=[
            jax.ShapeDtypeStruct((pairs, modes), F32),
            jax.ShapeDtypeStruct(object_field.shape, F32),
        ],
        in_specs=[vmem] * 7 + [hbm] * 2,
        out_specs=[vmem, vmem],
        scratch_shapes=[
            pltpu.VMEM((modes, g, g), BF),
            pltpu.VMEM((blocks, padded, g), BF),
            pltpu.VMEM((pairs, g, g), BF),
            pltpu.VMEM((pairs * BLK, padded), BF),
            pltpu.VMEM((pairs, g, g), F32),
            pltpu.VMEM((pairs, g, g), F32),
            pltpu.VMEM((patches, g, span), F32),
            pltpu.VMEM((pairs * BLK, blocks * g), BF),
            pltpu.VMEM((lane_blocks * g * BLK // span, pairs, span), F32),
            pltpu.VMEM((pairs, lane_blocks * g), F32),
            pltpu.VMEM((lane_blocks, pairs, g), F32),
            pltpu.VMEM((lane_blocks, pairs, g), F32),
            pltpu.VMEM((2, patches, rows, g), BF),
            pltpu.VMEM((2, n_frame, patches, rows, g), BF),
            pltpu.VMEM((n_frame, patches, rows, g), BF),
            pltpu.VMEM((n_frame, patches, rows, g), BF),
            pltpu.VMEM((8, g), F32),
            pltpu.VMEM((8, g), F32),
            pltpu.VMEM((n_frame, 8, g), F32),
            pltpu.VMEM((2, n_patch, 8, g), F32),
            dma((PARTS,)),
            dma(()),
            dma((2, 2)),
            dma((2,)),
            dma((3, 2)),
        ],
        compiler_params=pltpu.CompilerParams(
            collective_id=0, has_side_effects=True, vmem_limit_bytes=62 * 1024 * 1024
        ),
    )(
        coeffs.reshape(pairs, modes),
        object_field,
        pupil_mask,
        fwd,
        inv,
        jnp.asarray(expand, BF),
        jnp.asarray(expand.T, BF),
        observed.reshape(pairs, g, g),
        mode_basis,
    )
    return new_coeffs.reshape(coeffs.shape), new_object


def solution(mesh):
    in_specs = (
        P("frame", "patch", None),
        P("frame", "patch", None, None),
        P("patch", "frame", None),
        P(),
        P(),
    )
    out_specs = (P("frame", "patch", None), P("patch", "frame", None))
    run = functools.partial(local, mesh.shape["frame"], mesh.shape["patch"])
    return jax.shard_map(run, mesh=mesh, in_specs=in_specs, out_specs=out_specs, check_vma=False)
```

```python
import functools
import math

import jax
import jax.numpy as jnp
import numpy as np
from jax import lax
from jax.experimental import pallas as pl
from jax.experimental.pallas import tpu as pltpu
from jax.sharding import PartitionSpec as P

EPSILON = 1e-06
STEP_OBJECT = 0.1
STEP_COEFF = 0.2
CHUNK = 8
BLK = 8
PARTS = 10
LANES = 128
MESH = pl.DeviceIdType.MESH
BF = jnp.bfloat16
F32 = jnp.float32


def fit(even):
    f = np.cos((np.arange(4000) + 0.5) * (np.pi / 8000)) * 0.5
    target = np.sqrt(2.0) * (np.cos(np.pi * f) if even else np.sin(np.pi * f) / f)
    powers = np.stack([f ** (2 * k) for k in range(6 if even else 5)], axis=1)
    coef = np.linalg.lstsq(powers, target, rcond=None)[0]
    return [float(np.float32(v)) for v in coef]


SIN_COEF = fit(False)
COS_COEF = fit(True)


def horner(z, coef):
    acc = coef[-1] * z + coef[-2]
    for value in coef[-3::-1]:
        acc = acc * z + value
    return acc


def sincos(x):
    turns = x * (1.0 / (2.0 * math.pi))
    f = turns - jnp.round(turns)
    z = f * f
    s = f * horner(z, SIN_COEF)
    c = horner(z, COS_COEF)
    return s * c, 1.0 - s * s


def dot(a, b):
    return jnp.dot(a, b, preferred_element_type=F32)


def swap_blocks(m):
    n = LANES
    return jnp.concatenate(
        [
            jnp.concatenate([m[:n, :n], m[n:, :n]], axis=1),
            jnp.concatenate([m[:n, n:], m[n:, n:]], axis=1),
        ],
        axis=0,
    )


def stack(m):
    return jnp.concatenate([m[:, :LANES], m[:, LANES:]], axis=0)


def tables(extent):
    counter = np.arange(extent)
    angles = (counter[:, None] * counter[None, :] % extent).astype(np.float32) * np.float32(
        2.0 * math.pi / extent
    )
    c, s = np.cos(angles), np.sin(angles)
    fwd = np.block([[c, -s], [s, c]]).astype(np.float32)
    inv = np.block([[c, s], [-s, c]]).astype(np.float32)
    return jnp.asarray(fwd, F32).astype(BF), jnp.asarray(inv, F32).astype(BF)


def patch_steps(phases, mask, spec, observed, scale, tabs, emit_term, emit_slope):
    t1, t2, t1s, t2s = tabs
    g = LANES
    trig = [sincos(p) for p in phases]
    cos = jnp.concatenate([c * mask for s, c in trig], axis=1)
    sin = jnp.concatenate([s * mask for s, c in trig], axis=1)
    x = swap_blocks(jnp.concatenate([cos.astype(BF), sin.astype(BF)], axis=0))
    y = dot(x, t1)
    yield
    focal = dot(t2, swap_blocks(y.astype(BF)))
    yield
    fr, fi = focal[:g], focal[g:]
    spread = (fr * fr + fi * fi) * scale
    y = dot(stack(spread.astype(BF)), t1[:g])
    yield
    otf = dot(t2, swap_blocks(y.astype(BF)))
    yield
    otr, oti = otf[:g], otf[g:]
    sr = jnp.concatenate([spec[:, :g]] * 2, axis=1)
    si = jnp.concatenate([spec[:, g:]] * 2, axis=1)
    mr = (sr * otr - si * oti).astype(BF)
    mi = (sr * oti + si * otr).astype(BF)
    y = dot(swap_blocks(jnp.concatenate([mr, mi], axis=0)), t2)
    yield
    image = dot(t1s[:g], swap_blocks(y.astype(BF)))
    yield
    obs = jnp.concatenate([o.astype(F32) for o in observed], axis=1)
    residual = image - obs
    y = dot(stack(residual.astype(BF)), t1[:g])
    yield
    grad = dot(t2s, swap_blocks(y.astype(BF)))
    yield
    gr, gi = grad[:g], grad[g:]
    ar = (gr * otr + gi * oti).astype(BF)
    ai = (gi * otr - gr * oti).astype(BF)
    half = dot(swap_blocks(jnp.concatenate([ar, ai], axis=0)), t2)
    br = (gr * sr + gi * si).astype(BF)
    bi = (gi * sr - gr * si).astype(BF)
    y = dot(swap_blocks(jnp.concatenate([br, bi], axis=0)), t2)
    yield
    term = dot(t1[:g], stack((half[:g] + half[g:]).astype(BF)))
    spread_grad = dot(t1[:g], swap_blocks(y.astype(BF)))
    yield
    emit_term(term)
    factor = (2.0 * scale) * spread_grad
    fr, fi = (factor * fr).astype(BF), (factor * fi).astype(BF)
    y = dot(swap_blocks(jnp.concatenate([fr, fi], axis=0)), t2)
    yield
    field = dot(t1, swap_blocks(y.astype(BF)))
    yield
    emit_slope(field[g:] * cos - field[:g] * sin)


def interleave(work):
    waiting, running = list(work), []
    while waiting or running:
        running += waiting[:1]
        waiting = waiting[1:]
        running = [w for w in running if next(w, "done") is None]


def kernel(
    sizes,
    coeff_in,
    object_in,
    mask_in,
    fwd_in,
    inv_in,
    observed_hbm,
    basis_hbm,
    coeff_out,
    object_out,
    staged,
    basis,
    observed,
    rows_left,
    phase,
    phase_step,
    spectrum,
    slopes,
    wide,
    coeff_now,
    turned,
    kept,
    old,
    own_grad,
    expand,
    ag_send,
    ag_recv,
    rs_send,
    rs_recv,
    sc_send,
    sc_recv,
    steps,
    basis_sem,
    load_sem,
    ag_sem,
    rs_sem,
    sc_sem,
):
    frames, patches, modes, n_frame, n_patch, rows = sizes
    g = LANES
    pairs = frames * patches
    blocks = g // BLK
    depth = modes * BLK
    span = 2 * g
    groups = -(-depth // span)
    lane_blocks = -(-modes // g)
    part = modes // PARTS
    me = lax.axis_index("frame")
    my_patch = lax.axis_index("patch")

    loads = [
        pltpu.make_async_copy(
            basis_hbm.at[pl.ds(k * part, part)], staged.at[pl.ds(k * part, part)], basis_sem.at[k]
        )
        for k in range(PARTS)
    ]
    for load in loads:
        load.start()
    load_observed = pltpu.make_async_copy(observed_hbm, observed, load_sem)
    load_observed.start()

    others = [
        {"frame": lax.rem(me + k, n_frame), "patch": lax.rem(my_patch + m, n_patch)}
        for k in range(n_frame)
        for m in range(n_patch)
        if k or m
    ]
    barrier = pltpu.get_barrier_semaphore()
    for device in others:
        pl.semaphore_signal(barrier, inc=1, device_id=device, device_id_type=MESH)

    ag_send[0] = object_in[...].astype(BF)
    coeff_now[...] = jnp.zeros(coeff_now.shape, F32)
    coeff_now[:, 0:modes] = coeff_in[...]
    wide[...] = jnp.zeros(wide.shape, F32)
    basis[:, pl.ds(depth, groups * span - depth), :] = jnp.zeros(
        (blocks, groups * span - depth, g), BF
    )
    mask = mask_in[...].astype(F32)
    scale = 1.0 / (g * g * jnp.sum(mask))
    mode_of = lax.broadcasted_iota(jnp.int32, expand.shape, 0)
    row_lane = lax.broadcasted_iota(jnp.int32, expand.shape, 1)
    expand[...] = jnp.where(mode_of == row_lane // BLK, 1.0, 0.0).astype(BF)

    def send_all(src, dst, sem, devices):
        for device in devices:
            pltpu.make_async_remote_copy(
                src_ref=src(device),
                dst_ref=dst,
                send_sem=sem.at[0],
                recv_sem=sem.at[1],
                device_id=device,
                device_id_type=MESH,
            ).start()

    def wait_all(block, sem):
        both = pltpu.make_async_remote_copy(
            src_ref=block,
            dst_ref=block,
            send_sem=sem.at[0],
            recv_sem=sem.at[1],
            device_id={"frame": 0},
            device_id_type=MESH,
        )
        both.wait_recv()
        both.wait_send()

    frame_peers = [{"frame": lax.rem(me + k, n_frame)} for k in range(1, n_frame)]

    def half_of(at):
        return pl.ds(pl.multiple_of(at * CHUNK, CHUNK), CHUNK)

    def gather(it, at):
        send_all(
            lambda device: ag_send.at[it, half_of(at)],
            ag_recv.at[it, me, half_of(at)],
            ag_sem.at[it, at],
            frame_peers,
        )

    def scatter(at):
        send_all(
            lambda device: rs_send.at[device["frame"], half_of(at)],
            rs_recv.at[me, half_of(at)],
            rs_sem.at[at],
            frame_peers,
        )

    row_of = lax.broadcasted_iota(jnp.int32, (BLK, span), 0)
    lane_of = lax.rem(lax.broadcasted_iota(jnp.int32, (BLK, span), 1), BLK)
    diagonal = row_of == lane_of

    def left_rows(pieces):
        for k in range(lane_blocks):
            width = min(groups * span - k * g * BLK, g * BLK)
            values = dot(pieces[k].astype(BF), expand[:, :width])
            for b in range(width // span):
                cut = values[:, b * span : (b + 1) * span]
                cut = jnp.broadcast_to(cut[:, None, :], (pairs, BLK, span))
                cut = jnp.where(diagonal[None], cut, 0.0)
                first = k * g * BLK + b * span
                rows_left[:, first : first + span] = cut.reshape(pairs * BLK, span).astype(BF)

    def basis_products(out_ref, start, stop):
        lhs = rows_left[:, :depth]

        def block(at, carry):
            rhs = jnp.concatenate([basis[2 * at, :depth, :], basis[2 * at + 1, :depth, :]], axis=1)
            out = dot(lhs, rhs)
            first = pl.multiple_of(at * 2 * BLK, 2 * BLK)
            out_ref[:, pl.ds(first, BLK), :] = out[:, :g].reshape(pairs, BLK, g)
            out_ref[:, pl.ds(first + BLK, BLK), :] = out[:, g:].reshape(pairs, BLK, g)
            return carry

        lax.fori_loop(start, stop, block, 0, unroll=2)

    def relay(k):
        def block(b, carry):
            taken = staged[pl.ds(k * part, part), pl.ds(pl.multiple_of(b * 2 * BLK, 2 * BLK), 2 * BLK), :]
            taken = taken.astype(F32)
            for h in range(2):
                half = taken[:, h * BLK : (h + 1) * BLK].reshape(part * BLK, g)
                basis[2 * b + h, pl.ds(k * part * BLK, part * BLK), :] = half.astype(BF)
            return carry

        lax.fori_loop(0, blocks // 2, block, 0)

    def spectra(it, at):
        for u in range(0, CHUNK, 2):
            q = at * CHUNK + u
            pieces = [
                ag_recv[it, :, q + v].astype(F32).reshape(g, g).astype(BF) for v in range(2)
            ]
            left = dot(inv_in[:, :g], jnp.concatenate(pieces, axis=1))
            out = dot(swap_blocks(left.astype(BF)), fwd_in[...])
            spectrum[it, q] = out[:g]
            spectrum[it, q + 1] = out[g:]

    inverse = 1.0 / (g * g)

    def scalar_steps(it):
        wait_all(sc_recv.at[it, pl.ds(0, n_frame * n_patch - 1)], sc_sem.at[it])
        total = jnp.sum(sc_recv[it], axis=0)
        first = lax.broadcasted_iota(jnp.int32, total.shape, 1) < g // 2
        object_sq = jnp.sum(jnp.where(first, total, 0.0), keepdims=True)
        coeff_sq = jnp.sum(jnp.where(first, 0.0, total), keepdims=True)
        object_count = patches * rows * g * n_frame * n_patch
        coeff_count = pairs * modes * n_frame * n_patch
        object_rms = jnp.sqrt(object_sq / object_count + EPSILON)
        coeff_rms = jnp.sqrt(coeff_sq / coeff_count + EPSILON)
        return STEP_OBJECT / object_rms, STEP_COEFF / coeff_rms

    def patch_chunk(it, at, carry):
        wait_all(ag_recv.at[it, pl.ds(0, n_frame - 1), half_of(at)], ag_sem.at[it, at])
        spectra(it, at)
        if it == 1:

            @pl.when(at == 0)
            def _():
                object_step, coeff_step = scalar_steps(0)
                steps[0:1, :] = jnp.broadcast_to(object_step, (1, g))
                steps[1:2, :] = jnp.broadcast_to(coeff_step, (1, g))

        fwd, inv = fwd_in[...], inv_in[...]
        tabs = (fwd, inv, fwd * BF(inverse), inv * BF(inverse))
        done = []

        def one(q):
            def emit_term(term):
                rs_send[:, q] = term.reshape(n_frame, rows, g).astype(BF)
                done.append(q)
                if len(done) == CHUNK:
                    scatter(at)

            def emit_slope(slope):
                first = pl.multiple_of(q * frames * BLK, frames * BLK)
                for b in range(blocks):
                    cut = slope[b * BLK : (b + 1) * BLK]
                    cut = jnp.concatenate([cut[:, f * g : (f + 1) * g] for f in range(frames)], axis=0)
                    slopes[pl.ds(first, frames * BLK), b * g : (b + 1) * g] = cut.astype(BF)

            picks = [f * patches + q for f in range(frames)]
            phases = [phase[p] for p in picks]
            spec = spectrum[0, q]
            if it == 1:
                phases = [x - steps[1:2, :] * phase_step[p] for x, p in zip(phases, picks)]
                object_step = jnp.concatenate([steps[0:1, :]] * 2, axis=1)
                spec = spec - object_step * spectrum[1, q]
            return patch_steps(
                phases, mask, spec, [observed[p] for p in picks], scale, tabs, emit_term, emit_slope
            )

        interleave([one(at * CHUNK + u) for u in range(CHUNK)])
        return carry

    def coeff_products(start, stop):
        lhs = slopes[...]

        def group(at, carry):
            first = pl.multiple_of(at * span, span)
            rhs = jnp.concatenate([basis[b, pl.ds(first, span), :] for b in range(blocks)], axis=1)
            out = lax.dot_general(lhs, rhs, (((1,), (1,)), ((), ())), preferred_element_type=F32)
            out = jnp.where(diagonal[None], out.reshape(pairs, BLK, span), 0.0)
            wide[at] = jnp.sum(out, axis=1)
            return carry

        lax.fori_loop(start, stop, group, 0, unroll=2)

    def coeff_gradient():
        per = g * BLK // span
        rest = jnp.concatenate(
            [
                jnp.concatenate([wide[k * per + b] for b in range(per)], axis=1)
                for k in range(lane_blocks)
            ],
            axis=0,
        )
        total = 0.0
        for _ in range(3):
            low = rest.astype(BF)
            total = total + lax.dot_general(
                low, expand[...], (((1,), (1,)), ((), ())), preferred_element_type=F32
            )
            rest = rest - low.astype(F32)
        pieces = []
        for k in range(lane_blocks):
            turned[k] = total[k * pairs : (k + 1) * pairs]
            pieces.append(
                jnp.concatenate(
                    [turned[k, pl.ds(f, patches, stride=frames), :] for f in range(frames)], axis=0
                )
            )
        return pieces

    def sum_half(it, at):
        wait_all(rs_recv.at[pl.ds(0, n_frame - 1), half_of(at)], rs_sem.at[at])
        own = rs_send[me, half_of(at)].astype(F32)
        for k in range(1, n_frame):
            own = own + rs_recv[lax.rem(me + k, n_frame), half_of(at)].astype(F32)
        own_grad[half_of(at)] = own
        if it == 0:
            ag_send[1, half_of(at)] = own.astype(BF)
            ag_recv[1, me, half_of(at)] = own.astype(BF)

    def gradients(it):
        sum_half(it, 0)
        coeff_products(0, 2)
        if it == 0:
            gather(1, 0)
        coeff_products(2, groups)
        pieces = coeff_gradient()
        sum_half(it, 1)
        own = own_grad[...]
        object_row = jnp.sum(jnp.sum(own * own, axis=0), axis=0, keepdims=True)
        coeff_row = jnp.sum(sum(piece * piece for piece in pieces), axis=0, keepdims=True)
        first = lax.broadcasted_iota(jnp.int32, (1, g), 1) < g // 2
        object_row = object_row + pltpu.roll(object_row, g // 2, 1)
        coeff_row = coeff_row + pltpu.roll(coeff_row, g // 2, 1)
        row = jnp.where(first, object_row, coeff_row)
        sc_send[it] = row
        slot = me * n_patch + my_patch
        sc_recv[it, slot] = row
        for k in range(lane_blocks):
            kept[k] = pieces[k]
        send_all(lambda device: sc_send.at[it], sc_recv.at[it, slot], sc_sem.at[it], others)
        return pieces

    left_rows([coeff_now[:, k * g : (k + 1) * g] for k in range(lane_blocks)])
    ag_recv[0, me] = ag_send[0]
    pl.semaphore_wait(barrier, len(others))
    gather(0, 0)
    gather(0, 1)
    for k in range(PARTS):
        loads[k].wait()
        relay(k)
    basis_products(phase, 0, blocks // 2)
    load_observed.wait()
    lax.fori_loop(0, patches // CHUNK, functools.partial(patch_chunk, 0), 0)
    pieces = gradients(0)

    gather(1, 1)
    left_rows(pieces)
    object_out[...] = own_grad[...]
    for k in range(lane_blocks):
        old[k] = kept[k]
    basis_products(phase_step, 0, blocks // 2)
    lax.fori_loop(0, patches // CHUNK, functools.partial(patch_chunk, 1), 0)
    gradients(1)
    object_now = object_in[...] - steps[0:1, :][None] * object_out[...]
    object_step, coeff_step = scalar_steps(1)
    object_out[...] = object_now - object_step[None] * own_grad[...]
    for k in range(lane_blocks):
        width = min(g, modes - k * g)
        cut = slice(k * g, k * g + width)
        now = coeff_now[:, k * g : (k + 1) * g] - steps[1:2, :] * old[k]
        coeff_out[:, cut] = (now - coeff_step * kept[k])[:, :width]


def pass_on(coeff_in, object_in, coeff_out, object_out):
    coeff_out[...] = coeff_in[...]
    object_out[...] = object_in[...]


def local(n_frame, n_patch, coeffs, observed, object_field, mode_basis, pupil_mask):
    frames, patches, modes = coeffs.shape
    rows, g = object_field.shape[1:]
    pairs = frames * patches
    blocks = g // BLK
    span = 2 * g
    padded = -(-modes * BLK // span) * span
    lane_blocks = -(-modes // g)
    fwd, inv = tables(g)
    vmem = pl.BlockSpec(memory_space=pltpu.VMEM)
    hbm = pl.BlockSpec(memory_space=pl.ANY)
    dma = pltpu.SemaphoreType.DMA
    sizes = (frames, patches, modes, n_frame, n_patch, rows)
    new_coeffs, new_object = pl.pallas_call(
        functools.partial(kernel, sizes),
        out_shape=[
            jax.ShapeDtypeStruct((pairs, modes), F32),
            jax.ShapeDtypeStruct(object_field.shape, F32),
        ],
        in_specs=[vmem] * 5 + [hbm] * 2,
        out_specs=[vmem, vmem],
        scratch_shapes=[
            pltpu.VMEM((modes, g, g), BF),
            pltpu.VMEM((blocks, padded, g), BF),
            pltpu.VMEM((pairs, g, g), BF),
            pltpu.VMEM((pairs * BLK, padded), BF),
            pltpu.VMEM((pairs, g, g), F32),
            pltpu.VMEM((pairs, g, g), F32),
            pltpu.VMEM((2, patches, g, span), F32),
            pltpu.VMEM((pairs * BLK, blocks * g), BF),
            pltpu.VMEM((lane_blocks * g * BLK // span, pairs, span), F32),
            pltpu.VMEM((pairs, lane_blocks * g), F32),
            pltpu.VMEM((lane_blocks, pairs, g), F32),
            pltpu.VMEM((lane_blocks, pairs, g), F32),
            pltpu.VMEM((lane_blocks, pairs, g), F32),
            pltpu.VMEM((patches, rows, g), F32),
            pltpu.VMEM((g, g * BLK), BF),
            pltpu.VMEM((2, patches, rows, g), BF),
            pltpu.VMEM((2, n_frame, patches, rows, g), BF),
            pltpu.VMEM((n_frame, patches, rows, g), BF),
            pltpu.VMEM((n_frame, patches, rows, g), BF),
            pltpu.VMEM((2, 1, g), F32),
            pltpu.VMEM((2, n_frame * n_patch, 1, g), F32),
            pltpu.VMEM((8, g), F32),
            dma((PARTS,)),
            dma(()),
            dma((2, 2, 2)),
            dma((2, 2)),
            dma((2, 2)),
        ],
        compiler_params=pltpu.CompilerParams(
            collective_id=0, has_side_effects=True, vmem_limit_bytes=62 * 1024 * 1024
        ),
    )(
        coeffs.reshape(pairs, modes),
        object_field,
        pupil_mask,
        fwd,
        inv,
        observed.reshape(pairs, g, g),
        mode_basis,
    )
    new_coeffs, new_object = pl.pallas_call(
        pass_on,
        out_shape=[
            jax.ShapeDtypeStruct(new_coeffs.shape, F32),
            jax.ShapeDtypeStruct(new_object.shape, F32),
        ],
    )(new_coeffs, new_object)
    return new_coeffs.reshape(coeffs.shape), new_object


def solution(mesh):
    in_specs = (
        P("frame", "patch", None),
        P("frame", "patch", None, None),
        P("patch", "frame", None),
        P(),
        P(),
    )
    out_specs = (P("frame", "patch", None), P("patch", "frame", None))
    run = functools.partial(local, mesh.shape["frame"], mesh.shape["patch"])
    return jax.shard_map(run, mesh=mesh, in_specs=in_specs, out_specs=out_specs, check_vma=False)
```

```python
import functools
import math

import jax
import jax.numpy as jnp
import numpy as np
from jax import lax
from jax.experimental import pallas as pl
from jax.experimental.pallas import tpu as pltpu
from jax.sharding import PartitionSpec as P

EPSILON = 1e-06
STEP_OBJECT = 0.1
STEP_COEFF = 0.2
CHUNK = 8
BLK = 8
LANES = 128
MESH = pl.DeviceIdType.MESH
BF = jnp.bfloat16
F32 = jnp.float32


def fit(even):
    f = np.cos((np.arange(4000) + 0.5) * (np.pi / 8000)) * 0.5
    target = np.sqrt(2.0) * (np.cos(np.pi * f) if even else np.sin(np.pi * f) / f)
    powers = np.stack([f ** (2 * k) for k in range(6 if even else 5)], axis=1)
    coef = np.linalg.lstsq(powers, target, rcond=None)[0]
    return [float(np.float32(v)) for v in coef]


SIN_COEF = fit(False)
COS_COEF = fit(True)


def horner(z, coef):
    acc = coef[-1] * z + coef[-2]
    for value in coef[-3::-1]:
        acc = acc * z + value
    return acc


def sincos(x):
    turns = x * (1.0 / (2.0 * math.pi))
    f = turns - jnp.round(turns)
    z = f * f
    s = f * horner(z, SIN_COEF)
    c = horner(z, COS_COEF)
    return s * c, 1.0 - s * s


def dot(a, b):
    return jnp.dot(a, b, preferred_element_type=F32)


def swap_blocks(m):
    n = LANES
    return jnp.concatenate(
        [
            jnp.concatenate([m[:n, :n], m[n:, :n]], axis=1),
            jnp.concatenate([m[:n, n:], m[n:, n:]], axis=1),
        ],
        axis=0,
    )


def stack(m):
    return jnp.concatenate([m[:, :LANES], m[:, LANES:]], axis=0)


def tables(extent):
    counter = np.arange(extent)
    angles = (counter[:, None] * counter[None, :] % extent).astype(np.float32) * np.float32(
        2.0 * math.pi / extent
    )
    c, s = np.cos(angles), np.sin(angles)
    fwd = np.block([[c, -s], [s, c]]).astype(np.float32)
    inv = np.block([[c, s], [-s, c]]).astype(np.float32)
    return jnp.asarray(fwd, F32).astype(BF), jnp.asarray(inv, F32).astype(BF)


def patch_steps(phases, mask, spec_of, observed, scale, tabs, emit_term, emit_slope):
    t1, t2, t1s, t2s = tabs
    g = LANES
    trig = [sincos(p) for p in phases]
    cos = jnp.concatenate([c * mask for s, c in trig], axis=1)
    sin = jnp.concatenate([s * mask for s, c in trig], axis=1)
    x = swap_blocks(jnp.concatenate([cos.astype(BF), sin.astype(BF)], axis=0))
    y = dot(x, t1)
    yield
    focal = dot(t2, swap_blocks(y.astype(BF)))
    yield
    fr, fi = focal[:g], focal[g:]
    spread = (fr * fr + fi * fi) * scale
    y = dot(stack(spread.astype(BF)), t1[:g])
    yield
    otf = dot(t2, swap_blocks(y.astype(BF)))
    yield
    otr, oti = otf[:g], otf[g:]
    spec = spec_of()
    sr = jnp.concatenate([spec[:, :g]] * 2, axis=1)
    si = jnp.concatenate([spec[:, g:]] * 2, axis=1)
    mr = (sr * otr - si * oti).astype(BF)
    mi = (sr * oti + si * otr).astype(BF)
    y = dot(swap_blocks(jnp.concatenate([mr, mi], axis=0)), t2)
    yield
    image = dot(t1s[:g], swap_blocks(y.astype(BF)))
    yield
    obs = jnp.concatenate([o.astype(F32) for o in observed], axis=1)
    residual = image - obs
    y = dot(stack(residual.astype(BF)), t1[:g])
    yield
    grad = dot(t2s, swap_blocks(y.astype(BF)))
    yield
    gr, gi = grad[:g], grad[g:]
    ar = (gr * otr + gi * oti).astype(BF)
    ai = (gi * otr - gr * oti).astype(BF)
    half = dot(swap_blocks(jnp.concatenate([ar, ai], axis=0)), t2)
    br = (gr * sr + gi * si).astype(BF)
    bi = (gi * sr - gr * si).astype(BF)
    y = dot(swap_blocks(jnp.concatenate([br, bi], axis=0)), t2)
    yield
    term = dot(t1[:g], stack((half[:g] + half[g:]).astype(BF)))
    spread_grad = dot(t1[:g], swap_blocks(y.astype(BF)))
    yield
    emit_term(term)
    factor = (2.0 * scale) * spread_grad
    fr, fi = (factor * fr).astype(BF), (factor * fi).astype(BF)
    y = dot(swap_blocks(jnp.concatenate([fr, fi], axis=0)), t2)
    yield
    field = dot(t1, swap_blocks(y.astype(BF)))
    yield
    emit_slope(field[g:] * cos - field[:g] * sin)


def interleave(work):
    waiting, running = list(work), []
    while waiting or running:
        running += waiting[:1]
        waiting = waiting[1:]
        running = [w for w in running if next(w, "done") is None]


def far_first(n_frame, n_patch):
    def hops(shift):
        dz, dx, dc, dh, dy = shift
        across = 2 if dh > dx else (1 if dh or dx else 0)
        return min(dz, n_frame // 4 - dz) + min(dy, n_patch // 2 - dy) + across

    shifts = [
        (dz, dx, dc, dh, dy)
        for dz in range(n_frame // 4)
        for dx in range(2)
        for dc in range(2)
        for dh in range(2)
        for dy in range(n_patch // 2)
    ][1:]
    shifts.sort(key=lambda shift: -hops(shift))
    frame = [shift for shift in shifts if not (shift[3] or shift[4])]
    patch = [shift for shift in shifts if not (shift[0] or shift[1] or shift[2])]
    return frame, patch, shifts


def kernel(
    sizes,
    coeff_in,
    object_in,
    mask_in,
    fwd_in,
    inv_in,
    observed_hbm,
    basis_hbm,
    coeff_out,
    object_out,
    staged,
    basis,
    observed,
    rows_left,
    phase,
    phase_step,
    spectrum,
    slopes,
    wide,
    coeff_now,
    turned,
    kept,
    old,
    own_grad,
    expand,
    ag_send,
    ag_recv,
    rs_send,
    rs_recv,
    sc_send,
    sc_recv,
    steps,
    basis_sem,
    load_sem,
    ag_sem,
    rs_sem,
    sc_sem,
    joined,
):
    frames, patches, modes, n_frame, n_patch, rows = sizes
    g = LANES
    pairs = frames * patches
    blocks = g // BLK
    depth = modes * BLK
    span = 2 * g
    groups = -(-depth // span)
    lane_blocks = -(-modes // g)
    me = lax.axis_index("frame")
    my_patch = lax.axis_index("patch")
    frame_shifts, patch_shifts, all_shifts = far_first(n_frame, n_patch)

    def device_at(shift):
        dz, dx, dc, dh, dy = shift
        device = {}
        if dz or dx or dc:
            z, rest = lax.div(me, 4), lax.rem(me, 4)
            device["frame"] = (
                lax.rem(z + dz, n_frame // 4) * 4
                + lax.rem(lax.div(rest, 2) + dx, 2) * 2
                + lax.rem(rest + dc, 2)
            )
        if dh or dy:
            half, y = lax.div(my_patch, n_patch // 2), lax.rem(my_patch, n_patch // 2)
            device["patch"] = lax.rem(half + dh, 2) * (n_patch // 2) + lax.rem(y + dy, n_patch // 2)
        return device

    frame_peers = [device_at(shift) for shift in frame_shifts]
    patch_peers = [device_at(shift) for shift in patch_shifts]
    others = [device_at(shift) for shift in all_shifts]

    barrier = pltpu.get_barrier_semaphore()
    for device in patch_peers + frame_peers:
        pl.semaphore_signal(barrier, inc=1, device_id=device, device_id_type=MESH)

    loads = [
        pltpu.make_async_copy(
            basis_hbm.at[:, pl.ds(k * 2 * BLK, 2 * BLK), :], staged.at[k], basis_sem.at[k]
        )
        for k in range(blocks // 2)
    ]
    for load in loads:
        load.start()
    load_observed = pltpu.make_async_copy(observed_hbm, observed, load_sem)
    load_observed.start()

    ag_send[0] = object_in[...].astype(BF)
    coeff_now[...] = jnp.zeros(coeff_now.shape, F32)
    coeff_now[:, 0:modes] = coeff_in[...]
    wide[...] = jnp.zeros(wide.shape, F32)
    basis[:, pl.ds(depth, groups * span - depth), :] = jnp.zeros(
        (blocks, groups * span - depth, g), BF
    )
    mask = mask_in[...].astype(F32)
    scale = 1.0 / (g * g * jnp.sum(mask))
    mode_of = lax.broadcasted_iota(jnp.int32, expand.shape, 0)
    row_lane = lax.broadcasted_iota(jnp.int32, expand.shape, 1)
    expand[...] = jnp.where(mode_of == row_lane // BLK, 1.0, 0.0).astype(BF)

    def send_all(src, dst, sem, devices):
        for device in devices:
            pltpu.make_async_remote_copy(
                src_ref=src(device),
                dst_ref=dst,
                send_sem=sem.at[0],
                recv_sem=sem.at[1],
                device_id=device,
                device_id_type=MESH,
            ).start()

    def wait_all(block, sem):
        both = pltpu.make_async_remote_copy(
            src_ref=block,
            dst_ref=block,
            send_sem=sem.at[0],
            recv_sem=sem.at[1],
            device_id={"frame": 0},
            device_id_type=MESH,
        )
        both.wait_recv()
        both.wait_send()

    def half_of(at):
        return pl.ds(pl.multiple_of(at * CHUNK, CHUNK), CHUNK)

    def gather(it, at):
        send_all(
            lambda device: ag_send.at[it, half_of(at)],
            ag_recv.at[it, me, half_of(at)],
            ag_sem.at[it, at],
            frame_peers,
        )

    def scatter(at):
        send_all(
            lambda device: rs_send.at[device["frame"], half_of(at)],
            rs_recv.at[me, half_of(at)],
            rs_sem.at[at],
            frame_peers,
        )

    row_of = lax.broadcasted_iota(jnp.int32, (BLK, span), 0)
    lane_of = lax.rem(lax.broadcasted_iota(jnp.int32, (BLK, span), 1), BLK)
    diagonal = row_of == lane_of

    def left_rows(pieces):
        for k in range(lane_blocks):
            width = min(groups * span - k * g * BLK, g * BLK)
            values = dot(pieces[k].astype(BF), expand[:, :width])
            for b in range(width // span):
                cut = values[:, b * span : (b + 1) * span]
                cut = jnp.broadcast_to(cut[:, None, :], (pairs, BLK, span))
                cut = jnp.where(diagonal[None], cut, 0.0)
                first = k * g * BLK + b * span
                rows_left[:, first : first + span] = cut.reshape(pairs * BLK, span).astype(BF)

    def basis_product(out_ref, at):
        lhs = rows_left[:, :depth]
        rhs = jnp.concatenate([basis[2 * at, :depth, :], basis[2 * at + 1, :depth, :]], axis=1)
        out = dot(lhs, rhs)
        first = pl.multiple_of(at * 2 * BLK, 2 * BLK)
        out_ref[:, pl.ds(first, BLK), :] = out[:, :g].reshape(pairs, BLK, g)
        out_ref[:, pl.ds(first + BLK, BLK), :] = out[:, g:].reshape(pairs, BLK, g)

    def relay(k):
        taken = staged[k].astype(F32)
        for h in range(2):
            half = taken[:, h * BLK : (h + 1) * BLK].reshape(depth, g)
            basis[2 * k + h, pl.ds(0, depth), :] = half.astype(BF)

    def spectra(it, q):
        pieces = [ag_recv[it, :, q + v].astype(F32).reshape(g, g).astype(BF) for v in range(2)]
        left = dot(inv_in[:, :g], jnp.concatenate(pieces, axis=1))
        out = dot(swap_blocks(left.astype(BF)), fwd_in[...])
        spectrum[it, q] = out[:g]
        spectrum[it, q + 1] = out[g:]

    inverse = 1.0 / (g * g)

    def scalar_steps(it):
        wait_all(sc_recv.at[it, pl.ds(0, n_frame * n_patch - 1)], sc_sem.at[it])
        total = jnp.sum(sc_recv[it], axis=0)
        first = lax.broadcasted_iota(jnp.int32, total.shape, 1) < g // 2
        object_sq = jnp.sum(jnp.where(first, total, 0.0), keepdims=True)
        coeff_sq = jnp.sum(jnp.where(first, 0.0, total), keepdims=True)
        object_count = patches * rows * g * n_frame * n_patch
        coeff_count = pairs * modes * n_frame * n_patch
        object_rms = jnp.sqrt(object_sq / object_count + EPSILON)
        coeff_rms = jnp.sqrt(coeff_sq / coeff_count + EPSILON)
        return STEP_OBJECT / object_rms, STEP_COEFF / coeff_rms

    def patch_chunk(it, at, carry):
        wait_all(ag_recv.at[it, pl.ds(0, n_frame - 1), half_of(at)], ag_sem.at[it, at])
        for u in range(0, CHUNK, 2):
            spectra(it, at * CHUNK + u)
        if it == 1:

            @pl.when(at == 0)
            def _():
                object_step, coeff_step = scalar_steps(0)
                steps[0:1, :] = jnp.broadcast_to(object_step, (1, g))
                steps[1:2, :] = jnp.broadcast_to(coeff_step, (1, g))

        fwd, inv = fwd_in[...], inv_in[...]
        tabs = (fwd, inv, fwd * BF(inverse), inv * BF(inverse))
        done = []

        def one(u):
            q = at * CHUNK + u

            def spec_of():
                spec = spectrum[0, q]
                if it == 1:
                    object_step = jnp.concatenate([steps[0:1, :]] * 2, axis=1)
                    spec = spec - object_step * spectrum[1, q]
                return spec

            def emit_term(term):
                rs_send[:, q] = term.reshape(n_frame, rows, g).astype(BF)
                done.append(q)
                if len(done) == CHUNK:
                    scatter(at)

            def emit_slope(slope):
                first = pl.multiple_of(q * frames * BLK, frames * BLK)
                for b in range(blocks):
                    cut = slope[b * BLK : (b + 1) * BLK]
                    cut = jnp.concatenate([cut[:, f * g : (f + 1) * g] for f in range(frames)], axis=0)
                    slopes[pl.ds(first, frames * BLK), b * g : (b + 1) * g] = cut.astype(BF)

            picks = [f * patches + q for f in range(frames)]
            phases = [phase[p] for p in picks]
            if it == 1:
                phases = [x - steps[1:2, :] * phase_step[p] for x, p in zip(phases, picks)]
            return patch_steps(
                phases,
                mask,
                spec_of,
                [observed[p] for p in picks],
                scale,
                tabs,
                emit_term,
                emit_slope,
            )

        interleave([one(u) for u in range(CHUNK)])
        return carry

    def coeff_products(start, stop):
        lhs = slopes[...]

        def group(at, carry):
            first = pl.multiple_of(at * span, span)
            rhs = jnp.concatenate([basis[b, pl.ds(first, span), :] for b in range(blocks)], axis=1)
            out = lax.dot_general(lhs, rhs, (((1,), (1,)), ((), ())), preferred_element_type=F32)
            out = jnp.where(diagonal[None], out.reshape(pairs, BLK, span), 0.0)
            wide[at] = jnp.sum(out, axis=1)
            return carry

        lax.fori_loop(start, stop, group, 0, unroll=min(4, stop - start))

    def coeff_gradient():
        per = g * BLK // span
        rest = jnp.concatenate(
            [
                jnp.concatenate([wide[k * per + b] for b in range(per)], axis=1)
                for k in range(lane_blocks)
            ],
            axis=0,
        )
        total = 0.0
        for _ in range(3):
            low = rest.astype(BF)
            total = total + lax.dot_general(
                low, expand[...], (((1,), (1,)), ((), ())), preferred_element_type=F32
            )
            rest = rest - low.astype(F32)
        pieces = []
        for k in range(lane_blocks):
            turned[k] = total[k * pairs : (k + 1) * pairs]
            pieces.append(
                jnp.concatenate(
                    [turned[k, pl.ds(f, patches, stride=frames), :] for f in range(frames)], axis=0
                )
            )
        return pieces

    def sum_half(it, at):
        wait_all(rs_recv.at[pl.ds(0, n_frame - 1), half_of(at)], rs_sem.at[at])
        own = rs_send[me, half_of(at)].astype(F32)
        for k in range(1, n_frame):
            own = own + rs_recv[lax.rem(me + k, n_frame), half_of(at)].astype(F32)
        own_grad[half_of(at)] = own
        if it == 0:
            ag_send[1, half_of(at)] = own.astype(BF)
            ag_recv[1, me, half_of(at)] = own.astype(BF)

    def gradients(it):
        sum_half(it, 0)
        coeff_products(0, 2)
        if it == 0:
            gather(1, 0)
        coeff_products(2, groups)
        pieces = coeff_gradient()
        sum_half(it, 1)
        own = own_grad[...]
        object_row = jnp.sum(jnp.sum(own * own, axis=0), axis=0, keepdims=True)
        coeff_row = jnp.sum(sum(piece * piece for piece in pieces), axis=0, keepdims=True)
        first = lax.broadcasted_iota(jnp.int32, (1, g), 1) < g // 2
        object_row = object_row + pltpu.roll(object_row, g // 2, 1)
        coeff_row = coeff_row + pltpu.roll(coeff_row, g // 2, 1)
        row = jnp.where(first, object_row, coeff_row)
        sc_send[it] = row
        slot = me * n_patch + my_patch
        sc_recv[it, slot] = row
        for k in range(lane_blocks):
            kept[k] = pieces[k]
        if it == 0:
            pl.semaphore_wait(joined, len(patch_peers))
        send_all(lambda device: sc_send.at[it], sc_recv.at[it, slot], sc_sem.at[it], others)
        return pieces

    left_rows([coeff_now[:, k * g : (k + 1) * g] for k in range(lane_blocks)])
    ag_recv[0, me] = ag_send[0]
    for k in range(blocks // 2):
        loads[k].wait()
        relay(k)
        if k >= 1:
            basis_product(phase, k - 1)
        if k == 1:
            pl.semaphore_wait(barrier, len(patch_peers + frame_peers))
            gather(0, 0)
            gather(0, 1)
            for device in patch_peers:
                pl.semaphore_signal(joined, inc=1, device_id=device, device_id_type=MESH)
    basis_product(phase, blocks // 2 - 1)
    load_observed.wait()
    lax.fori_loop(0, patches // CHUNK, functools.partial(patch_chunk, 0), 0)
    pieces = gradients(0)

    gather(1, 1)
    left_rows(pieces)
    object_out[...] = own_grad[...]
    for k in range(lane_blocks):
        old[k] = kept[k]

    def step_product(at, carry):
        basis_product(phase_step, at)
        return carry

    lax.fori_loop(0, blocks // 2, step_product, 0, unroll=4)
    lax.fori_loop(0, patches // CHUNK, functools.partial(patch_chunk, 1), 0)
    gradients(1)
    object_now = object_in[...] - steps[0:1, :][None] * object_out[...]
    object_step, coeff_step = scalar_steps(1)
    object_out[...] = object_now - object_step[None] * own_grad[...]
    for k in range(lane_blocks):
        width = min(g, modes - k * g)
        cut = slice(k * g, k * g + width)
        now = coeff_now[:, k * g : (k + 1) * g] - steps[1:2, :] * old[k]
        coeff_out[:, cut] = (now - coeff_step * kept[k])[:, :width]


def pass_on(coeff_in, object_in, coeff_out, object_out):
    coeff_out[...] = coeff_in[...]
    object_out[...] = object_in[...]


def local(n_frame, n_patch, coeffs, observed, object_field, mode_basis, pupil_mask):
    frames, patches, modes = coeffs.shape
    rows, g = object_field.shape[1:]
    pairs = frames * patches
    blocks = g // BLK
    span = 2 * g
    padded = -(-modes * BLK // span) * span
    lane_blocks = -(-modes // g)
    fwd, inv = tables(g)
    vmem = pl.BlockSpec(memory_space=pltpu.VMEM)
    hbm = pl.BlockSpec(memory_space=pl.ANY)
    dma = pltpu.SemaphoreType.DMA
    sizes = (frames, patches, modes, n_frame, n_patch, rows)
    new_coeffs, new_object = pl.pallas_call(
        functools.partial(kernel, sizes),
        out_shape=[
            jax.ShapeDtypeStruct((pairs, modes), F32),
            jax.ShapeDtypeStruct(object_field.shape, F32),
        ],
        in_specs=[vmem] * 5 + [hbm] * 2,
        out_specs=[vmem, vmem],
        scratch_shapes=[
            pltpu.VMEM((blocks // 2, modes, 2 * BLK, g), BF),
            pltpu.VMEM((blocks, padded, g), BF),
            pltpu.VMEM((pairs, g, g), BF),
            pltpu.VMEM((pairs * BLK, padded), BF),
            pltpu.VMEM((pairs, g, g), F32),
            pltpu.VMEM((pairs, g, g), F32),
            pltpu.VMEM((2, patches, g, span), F32),
            pltpu.VMEM((pairs * BLK, blocks * g), BF),
            pltpu.VMEM((lane_blocks * g * BLK // span, pairs, span), F32),
            pltpu.VMEM((pairs, lane_blocks * g), F32),
            pltpu.VMEM((lane_blocks, pairs, g), F32),
            pltpu.VMEM((lane_blocks, pairs, g), F32),
            pltpu.VMEM((lane_blocks, pairs, g), F32),
            pltpu.VMEM((patches, rows, g), F32),
            pltpu.VMEM((g, g * BLK), BF),
            pltpu.VMEM((2, patches, rows, g), BF),
            pltpu.VMEM((2, n_frame, patches, rows, g), BF),
            pltpu.VMEM((n_frame, patches, rows, g), BF),
            pltpu.VMEM((n_frame, patches, rows, g), BF),
            pltpu.VMEM((2, 1, g), F32),
            pltpu.VMEM((2, n_frame * n_patch, 1, g), F32),
            pltpu.VMEM((8, g), F32),
            dma((blocks // 2,)),
            dma(()),
            dma((2, 2, 2)),
            dma((2, 2)),
            dma((2, 2)),
            pltpu.SemaphoreType.REGULAR,
        ],
        compiler_params=pltpu.CompilerParams(
            collective_id=0, has_side_effects=True, vmem_limit_bytes=62 * 1024 * 1024
        ),
    )(
        coeffs.reshape(pairs, modes),
        object_field,
        pupil_mask,
        fwd,
        inv,
        observed.reshape(pairs, g, g),
        mode_basis,
    )
    new_coeffs, new_object = pl.pallas_call(
        pass_on,
        out_shape=[
            jax.ShapeDtypeStruct(new_coeffs.shape, F32),
            jax.ShapeDtypeStruct(new_object.shape, F32),
        ],
    )(new_coeffs, new_object)
    return new_coeffs.reshape(coeffs.shape), new_object


def solution(mesh):
    in_specs = (
        P("frame", "patch", None),
        P("frame", "patch", None, None),
        P("patch", "frame", None),
        P(),
        P(),
    )
    out_specs = (P("frame", "patch", None), P("patch", "frame", None))
    run = functools.partial(local, mesh.shape["frame"], mesh.shape["patch"])
    return jax.shard_map(run, mesh=mesh, in_specs=in_specs, out_specs=out_specs, check_vma=False)
```

```python
import functools
import math

import jax
import jax.numpy as jnp
import numpy as np
from jax import lax
from jax.experimental import pallas as pl
from jax.experimental.pallas import tpu as pltpu
from jax.sharding import PartitionSpec as P

EPSILON = 1e-06
STEP_OBJECT = 0.1
STEP_COEFF = 0.2
CHUNK = 8
BLK = 8
LANES = 128
MESH = pl.DeviceIdType.MESH
BF = jnp.bfloat16
F32 = jnp.float32


def fit(even):
    f = np.cos((np.arange(4000) + 0.5) * (np.pi / 8000)) * 0.5
    target = np.sqrt(2.0) * (np.cos(np.pi * f) if even else np.sin(np.pi * f) / f)
    powers = np.stack([f ** (2 * k) for k in range(6 if even else 5)], axis=1)
    coef = np.linalg.lstsq(powers, target, rcond=None)[0]
    return [float(np.float32(v)) for v in coef]


SIN_COEF = fit(False)
COS_COEF = fit(True)


def horner(z, coef):
    acc = coef[-1] * z + coef[-2]
    for value in coef[-3::-1]:
        acc = acc * z + value
    return acc


def sincos(x):
    turns = x * (1.0 / (2.0 * math.pi))
    f = turns - jnp.round(turns)
    z = f * f
    s = f * horner(z, SIN_COEF)
    c = horner(z, COS_COEF)
    return s * c, 1.0 - s * s


def dot(a, b):
    return jnp.dot(a, b, preferred_element_type=F32)


def swap_blocks(m):
    n = LANES
    return jnp.concatenate(
        [
            jnp.concatenate([m[:n, :n], m[n:, :n]], axis=1),
            jnp.concatenate([m[:n, n:], m[n:, n:]], axis=1),
        ],
        axis=0,
    )


def stack(m):
    return jnp.concatenate([m[:, :LANES], m[:, LANES:]], axis=0)


def tables(extent):
    counter = np.arange(extent)
    angles = (counter[:, None] * counter[None, :] % extent).astype(np.float32) * np.float32(
        2.0 * math.pi / extent
    )
    c, s = np.cos(angles), np.sin(angles)
    fwd = np.block([[c, -s], [s, c]]).astype(np.float32)
    inv = np.block([[c, s], [-s, c]]).astype(np.float32)
    return jnp.asarray(fwd, F32).astype(BF), jnp.asarray(inv, F32).astype(BF)


def patch_steps(phases, mask, spec_of, observed, scale, tabs, emit_term, emit_slope):
    t1, t2, t1s, t2s = tabs
    g = LANES
    trig = [sincos(p) for p in phases]
    cos = jnp.concatenate([c * mask for s, c in trig], axis=1)
    sin = jnp.concatenate([s * mask for s, c in trig], axis=1)
    x = swap_blocks(jnp.concatenate([cos.astype(BF), sin.astype(BF)], axis=0))
    y = dot(x, t1)
    yield
    focal = dot(t2, swap_blocks(y.astype(BF)))
    yield
    fr, fi = focal[:g], focal[g:]
    spread = (fr * fr + fi * fi) * scale
    y = dot(stack(spread.astype(BF)), t1[:g])
    yield
    otf = dot(t2, swap_blocks(y.astype(BF)))
    yield
    otr, oti = otf[:g], otf[g:]
    spec = spec_of()
    sr = jnp.concatenate([spec[:, :g]] * 2, axis=1)
    si = jnp.concatenate([spec[:, g:]] * 2, axis=1)
    mr = (sr * otr - si * oti).astype(BF)
    mi = (sr * oti + si * otr).astype(BF)
    y = dot(swap_blocks(jnp.concatenate([mr, mi], axis=0)), t2)
    yield
    image = dot(t1s[:g], swap_blocks(y.astype(BF)))
    yield
    obs = jnp.concatenate([o.astype(F32) for o in observed], axis=1)
    residual = image - obs
    y = dot(stack(residual.astype(BF)), t1[:g])
    yield
    grad = dot(t2s, swap_blocks(y.astype(BF)))
    yield
    gr, gi = grad[:g], grad[g:]
    ar = (gr * otr + gi * oti).astype(BF)
    ai = (gi * otr - gr * oti).astype(BF)
    half = dot(swap_blocks(jnp.concatenate([ar, ai], axis=0)), t2)
    br = (gr * sr + gi * si).astype(BF)
    bi = (gi * sr - gr * si).astype(BF)
    y = dot(swap_blocks(jnp.concatenate([br, bi], axis=0)), t2)
    yield
    term = dot(t1[:g], stack((half[:g] + half[g:]).astype(BF)))
    spread_grad = dot(t1[:g], swap_blocks(y.astype(BF)))
    yield
    emit_term(term)
    factor = (2.0 * scale) * spread_grad
    fr, fi = (factor * fr).astype(BF), (factor * fi).astype(BF)
    y = dot(swap_blocks(jnp.concatenate([fr, fi], axis=0)), t2)
    yield
    field = dot(t1, swap_blocks(y.astype(BF)))
    yield
    emit_slope(field[g:] * cos - field[:g] * sin)


def interleave(work):
    waiting, running = list(work), []
    while waiting or running:
        running += waiting[:1]
        waiting = waiting[1:]
        running = [w for w in running if next(w, "done") is None]


def far_first(n_frame, n_patch):
    def hops(shift):
        dz, dx, dc, dh, dy = shift
        across = 2 if dh > dx else (1 if dh or dx else 0)
        return min(dz, n_frame // 4 - dz) + min(dy, n_patch // 2 - dy) + across

    shifts = [
        (dz, dx, dc, dh, dy)
        for dz in range(n_frame // 4)
        for dx in range(2)
        for dc in range(2)
        for dh in range(2)
        for dy in range(n_patch // 2)
    ][1:]
    shifts.sort(key=lambda shift: -hops(shift))
    frame = [shift for shift in shifts if not (shift[3] or shift[4])]
    patch = [shift for shift in shifts if not (shift[0] or shift[1] or shift[2])]
    return frame, patch, shifts


def kernel(
    sizes,
    coeff_in,
    object_in,
    mask_in,
    fwd_in,
    inv_in,
    observed_hbm,
    basis_hbm,
    coeff_out,
    object_out,
    staged,
    basis,
    observed,
    rows_left,
    phase,
    phase_step,
    spectrum,
    slopes,
    wide,
    coeff_now,
    turned,
    kept,
    old,
    own_grad,
    expand,
    ag_send,
    ag_recv,
    rs_send,
    rs_recv,
    sc_send,
    sc_recv,
    steps,
    basis_sem,
    load_sem,
    ag_sem,
    rs_sem,
    sc_sem,
    joined,
):
    frames, patches, modes, n_frame, n_patch, rows = sizes
    g = LANES
    pairs = frames * patches
    blocks = g // BLK
    depth = modes * BLK
    span = 2 * g
    groups = -(-depth // span)
    lane_blocks = -(-modes // g)
    me = lax.axis_index("frame")
    my_patch = lax.axis_index("patch")
    frame_shifts, patch_shifts, all_shifts = far_first(n_frame, n_patch)

    z, rest = lax.div(me, 4), lax.rem(me, 4)
    half, y = lax.div(my_patch, n_patch // 2), lax.rem(my_patch, n_patch // 2)
    x, core = lax.div(rest, 2), lax.rem(rest, 2)
    z_at = [z * 4] + [lax.rem(z + d, n_frame // 4) * 4 for d in range(1, n_frame // 4)]
    x_at, core_at = [x * 2, 2 - x * 2], [core, 1 - core]
    half_at = [half * (n_patch // 2), (1 - half) * (n_patch // 2)]
    y_at = [y] + [lax.rem(y + d, n_patch // 2) for d in range(1, n_patch // 2)]
    frame_at = {
        (dz, dx, dc): z_at[dz] + x_at[dx] + core_at[dc]
        for dz in range(n_frame // 4)
        for dx in range(2)
        for dc in range(2)
    }
    patch_at = {(dh, dy): half_at[dh] + y_at[dy] for dh in range(2) for dy in range(n_patch // 2)}

    def device_at(shift):
        device = {}
        if any(shift[:3]):
            device["frame"] = frame_at[shift[:3]]
        if any(shift[3:]):
            device["patch"] = patch_at[shift[3:]]
        return device

    frame_peers = [device_at(shift) for shift in frame_shifts]
    patch_peers = [device_at(shift) for shift in patch_shifts]
    others = [device_at(shift) for shift in all_shifts]

    barrier = pltpu.get_barrier_semaphore()
    for device in patch_peers + frame_peers:
        pl.semaphore_signal(barrier, inc=1, device_id=device, device_id_type=MESH)

    loads = [
        pltpu.make_async_copy(
            basis_hbm.at[:, pl.ds(k * 2 * BLK, 2 * BLK), :], staged.at[k], basis_sem.at[k]
        )
        for k in range(blocks // 2)
    ]
    for load in loads:
        load.start()
    load_observed = pltpu.make_async_copy(observed_hbm, observed, load_sem)
    load_observed.start()

    ag_send[0] = object_in[...].astype(BF)
    coeff_now[...] = jnp.zeros(coeff_now.shape, F32)
    coeff_now[:, 0:modes] = coeff_in[...]
    wide[...] = jnp.zeros(wide.shape, F32)
    basis[:, pl.ds(depth, groups * span - depth), :] = jnp.zeros(
        (blocks, groups * span - depth, g), BF
    )
    mask = mask_in[...].astype(F32)
    scale = 1.0 / (g * g * jnp.sum(mask))
    mode_of = lax.broadcasted_iota(jnp.int32, expand.shape, 0)
    row_lane = lax.broadcasted_iota(jnp.int32, expand.shape, 1)
    expand[...] = jnp.where(mode_of == row_lane // BLK, 1.0, 0.0).astype(BF)

    def send_all(src, dst, sem, devices):
        for device in devices:
            pltpu.make_async_remote_copy(
                src_ref=src(device),
                dst_ref=dst,
                send_sem=sem.at[0],
                recv_sem=sem.at[1],
                device_id=device,
                device_id_type=MESH,
            ).start()

    def wait_all(block, sem):
        both = pltpu.make_async_remote_copy(
            src_ref=block,
            dst_ref=block,
            send_sem=sem.at[0],
            recv_sem=sem.at[1],
            device_id={"frame": 0},
            device_id_type=MESH,
        )
        both.wait_recv()
        both.wait_send()

    def half_of(at):
        return pl.ds(pl.multiple_of(at * CHUNK, CHUNK), CHUNK)

    def gather(it, at):
        send_all(
            lambda device: ag_send.at[it, half_of(at)],
            ag_recv.at[it, me, half_of(at)],
            ag_sem.at[it, at],
            frame_peers,
        )

    def scatter(at):
        send_all(
            lambda device: rs_send.at[device["frame"], half_of(at)],
            rs_recv.at[me, half_of(at)],
            rs_sem.at[at],
            frame_peers,
        )

    row_of = lax.broadcasted_iota(jnp.int32, (BLK, span), 0)
    lane_of = lax.rem(lax.broadcasted_iota(jnp.int32, (BLK, span), 1), BLK)
    diagonal = row_of == lane_of

    def left_rows(pieces):
        for k in range(lane_blocks):
            width = min(groups * span - k * g * BLK, g * BLK)
            values = dot(pieces[k].astype(BF), expand[:, :width])
            for b in range(width // span):
                cut = values[:, b * span : (b + 1) * span]
                cut = jnp.broadcast_to(cut[:, None, :], (pairs, BLK, span))
                cut = jnp.where(diagonal[None], cut, 0.0)
                first = k * g * BLK + b * span
                rows_left[:, first : first + span] = cut.reshape(pairs * BLK, span).astype(BF)

    def basis_product(out_ref, at):
        lhs = rows_left[:, :depth]
        rhs = jnp.concatenate([basis[2 * at, :depth, :], basis[2 * at + 1, :depth, :]], axis=1)
        out = dot(lhs, rhs)
        first = pl.multiple_of(at * 2 * BLK, 2 * BLK)
        out_ref[:, pl.ds(first, BLK), :] = out[:, :g].reshape(pairs, BLK, g)
        out_ref[:, pl.ds(first + BLK, BLK), :] = out[:, g:].reshape(pairs, BLK, g)

    def relay(k):
        taken = staged[k].astype(F32)
        for h in range(2):
            half = taken[:, h * BLK : (h + 1) * BLK].reshape(depth, g)
            basis[2 * k + h, pl.ds(0, depth), :] = half.astype(BF)

    def spectra(it, q):
        pieces = [ag_recv[it, :, q + v].astype(F32).reshape(g, g).astype(BF) for v in range(2)]
        left = dot(inv_in[:, :g], jnp.concatenate(pieces, axis=1))
        out = dot(swap_blocks(left.astype(BF)), fwd_in[...])
        spectrum[it, q] = out[:g]
        spectrum[it, q + 1] = out[g:]

    inverse = 1.0 / (g * g)

    def scalar_steps(it):
        wait_all(sc_recv.at[it, pl.ds(0, n_frame * n_patch - 1)], sc_sem.at[it])
        total = jnp.sum(sc_recv[it], axis=0)
        first = lax.broadcasted_iota(jnp.int32, total.shape, 1) < g // 2
        object_sq = jnp.sum(jnp.where(first, total, 0.0), keepdims=True)
        coeff_sq = jnp.sum(jnp.where(first, 0.0, total), keepdims=True)
        object_count = patches * rows * g * n_frame * n_patch
        coeff_count = pairs * modes * n_frame * n_patch
        object_rms = jnp.sqrt(object_sq / object_count + EPSILON)
        coeff_rms = jnp.sqrt(coeff_sq / coeff_count + EPSILON)
        return STEP_OBJECT / object_rms, STEP_COEFF / coeff_rms

    def patch_chunk(it, at, carry):
        wait_all(ag_recv.at[it, pl.ds(0, n_frame - 1), half_of(at)], ag_sem.at[it, at])
        for u in range(0, CHUNK, 2):
            spectra(it, at * CHUNK + u)
        if it == 1:

            @pl.when(at == 0)
            def _():
                object_step, coeff_step = scalar_steps(0)
                steps[0:1, :] = jnp.broadcast_to(object_step, (1, g))
                steps[1:2, :] = jnp.broadcast_to(coeff_step, (1, g))

        fwd, inv = fwd_in[...], inv_in[...]
        tabs = (fwd, inv, fwd * BF(inverse), inv * BF(inverse))
        done = []

        def one(u):
            q = at * CHUNK + u

            def spec_of():
                spec = spectrum[0, q]
                if it == 1:
                    object_step = jnp.concatenate([steps[0:1, :]] * 2, axis=1)
                    spec = spec - object_step * spectrum[1, q]
                return spec

            def emit_term(term):
                rs_send[:, q] = term.reshape(n_frame, rows, g).astype(BF)
                done.append(q)
                if len(done) == CHUNK:
                    scatter(at)

            def emit_slope(slope):
                first = pl.multiple_of(q * frames * BLK, frames * BLK)
                for b in range(blocks):
                    cut = slope[b * BLK : (b + 1) * BLK]
                    cut = jnp.concatenate([cut[:, f * g : (f + 1) * g] for f in range(frames)], axis=0)
                    slopes[pl.ds(first, frames * BLK), b * g : (b + 1) * g] = cut.astype(BF)

            picks = [f * patches + q for f in range(frames)]
            phases = [phase[p] for p in picks]
            if it == 1:
                phases = [x - steps[1:2, :] * phase_step[p] for x, p in zip(phases, picks)]
            return patch_steps(
                phases,
                mask,
                spec_of,
                [observed[p] for p in picks],
                scale,
                tabs,
                emit_term,
                emit_slope,
            )

        interleave([one(u) for u in range(CHUNK)])
        return carry

    def coeff_products(start, stop):
        lhs = slopes[...]

        def group(at, carry):
            first = pl.multiple_of(at * span, span)
            rhs = jnp.concatenate([basis[b, pl.ds(first, span), :] for b in range(blocks)], axis=1)
            out = lax.dot_general(lhs, rhs, (((1,), (1,)), ((), ())), preferred_element_type=F32)
            out = jnp.where(diagonal[None], out.reshape(pairs, BLK, span), 0.0)
            wide[at] = jnp.sum(out, axis=1)
            return carry

        lax.fori_loop(start, stop, group, 0, unroll=min(8, stop - start))

    def coeff_gradient():
        per = g * BLK // span
        rest = jnp.concatenate(
            [
                jnp.concatenate([wide[k * per + b] for b in range(per)], axis=1)
                for k in range(lane_blocks)
            ],
            axis=0,
        )
        total = 0.0
        for _ in range(3):
            low = rest.astype(BF)
            total = total + lax.dot_general(
                low, expand[...], (((1,), (1,)), ((), ())), preferred_element_type=F32
            )
            rest = rest - low.astype(F32)
        pieces = []
        for k in range(lane_blocks):
            turned[k] = total[k * pairs : (k + 1) * pairs]
            pieces.append(
                jnp.concatenate(
                    [turned[k, pl.ds(f, patches, stride=frames), :] for f in range(frames)], axis=0
                )
            )
        return pieces

    def sum_half(it, at):
        wait_all(rs_recv.at[pl.ds(0, n_frame - 1), half_of(at)], rs_sem.at[at])
        own = rs_send[me, half_of(at)].astype(F32)
        for k in range(1, n_frame):
            own = own + rs_recv[lax.rem(me + k, n_frame), half_of(at)].astype(F32)
        own_grad[half_of(at)] = own
        if it == 0:
            ag_send[1, half_of(at)] = own.astype(BF)
            ag_recv[1, me, half_of(at)] = own.astype(BF)

    def gradients(it):
        sum_half(it, 0)
        coeff_products(0, 2)
        if it == 0:
            gather(1, 0)
        coeff_products(2, groups)
        pieces = coeff_gradient()
        sum_half(it, 1)
        own = own_grad[...]
        object_row = jnp.sum(jnp.sum(own * own, axis=0), axis=0, keepdims=True)
        coeff_row = jnp.sum(sum(piece * piece for piece in pieces), axis=0, keepdims=True)
        first = lax.broadcasted_iota(jnp.int32, (1, g), 1) < g // 2
        object_row = object_row + pltpu.roll(object_row, g // 2, 1)
        coeff_row = coeff_row + pltpu.roll(coeff_row, g // 2, 1)
        row = jnp.where(first, object_row, coeff_row)
        sc_send[it] = row
        slot = me * n_patch + my_patch
        sc_recv[it, slot] = row
        for k in range(lane_blocks):
            kept[k] = pieces[k]
        if it == 0:
            pl.semaphore_wait(joined, len(patch_peers))
        send_all(lambda device: sc_send.at[it], sc_recv.at[it, slot], sc_sem.at[it], others)
        return pieces

    left_rows([coeff_now[:, k * g : (k + 1) * g] for k in range(lane_blocks)])
    ag_recv[0, me] = ag_send[0]
    for k in range(blocks // 2):
        loads[k].wait()
        relay(k)
        if k >= 1:
            basis_product(phase, k - 1)
        if k == 1:
            pl.semaphore_wait(barrier, len(patch_peers + frame_peers))
            gather(0, 0)
            gather(0, 1)
            for device in patch_peers:
                pl.semaphore_signal(joined, inc=1, device_id=device, device_id_type=MESH)
    basis_product(phase, blocks // 2 - 1)
    load_observed.wait()
    lax.fori_loop(0, patches // CHUNK, functools.partial(patch_chunk, 0), 0)
    pieces = gradients(0)

    gather(1, 1)
    left_rows(pieces)
    object_out[...] = own_grad[...]
    for k in range(lane_blocks):
        old[k] = kept[k]

    def step_product(at, carry):
        basis_product(phase_step, at)
        return carry

    lax.fori_loop(0, blocks // 2, step_product, 0, unroll=8)
    lax.fori_loop(0, patches // CHUNK, functools.partial(patch_chunk, 1), 0)
    gradients(1)
    object_now = object_in[...] - steps[0:1, :][None] * object_out[...]
    object_step, coeff_step = scalar_steps(1)
    object_out[...] = object_now - object_step[None] * own_grad[...]
    for k in range(lane_blocks):
        width = min(g, modes - k * g)
        cut = slice(k * g, k * g + width)
        now = coeff_now[:, k * g : (k + 1) * g] - steps[1:2, :] * old[k]
        coeff_out[:, cut] = (now - coeff_step * kept[k])[:, :width]


def pass_on(coeff_in, object_in, coeff_out, object_out):
    coeff_out[...] = coeff_in[...]
    object_out[...] = object_in[...]


def local(n_frame, n_patch, coeffs, observed, object_field, mode_basis, pupil_mask):
    frames, patches, modes = coeffs.shape
    rows, g = object_field.shape[1:]
    pairs = frames * patches
    blocks = g // BLK
    span = 2 * g
    padded = -(-modes * BLK // span) * span
    lane_blocks = -(-modes // g)
    fwd, inv = tables(g)
    vmem = pl.BlockSpec(memory_space=pltpu.VMEM)
    hbm = pl.BlockSpec(memory_space=pl.ANY)
    dma = pltpu.SemaphoreType.DMA
    sizes = (frames, patches, modes, n_frame, n_patch, rows)
    new_coeffs, new_object = pl.pallas_call(
        functools.partial(kernel, sizes),
        out_shape=[
            jax.ShapeDtypeStruct((pairs, modes), F32),
            jax.ShapeDtypeStruct(object_field.shape, F32),
        ],
        in_specs=[vmem] * 5 + [hbm] * 2,
        out_specs=[vmem, vmem],
        scratch_shapes=[
            pltpu.VMEM((blocks // 2, modes, 2 * BLK, g), BF),
            pltpu.VMEM((blocks, padded, g), BF),
            pltpu.VMEM((pairs, g, g), BF),
            pltpu.VMEM((pairs * BLK, padded), BF),
            pltpu.VMEM((pairs, g, g), F32),
            pltpu.VMEM((pairs, g, g), F32),
            pltpu.VMEM((2, patches, g, span), F32),
            pltpu.VMEM((pairs * BLK, blocks * g), BF),
            pltpu.VMEM((lane_blocks * g * BLK // span, pairs, span), F32),
            pltpu.VMEM((pairs, lane_blocks * g), F32),
            pltpu.VMEM((lane_blocks, pairs, g), F32),
            pltpu.VMEM((lane_blocks, pairs, g), F32),
            pltpu.VMEM((lane_blocks, pairs, g), F32),
            pltpu.VMEM((patches, rows, g), F32),
            pltpu.VMEM((g, g * BLK), BF),
            pltpu.VMEM((2, patches, rows, g), BF),
            pltpu.VMEM((2, n_frame, patches, rows, g), BF),
            pltpu.VMEM((n_frame, patches, rows, g), BF),
            pltpu.VMEM((n_frame, patches, rows, g), BF),
            pltpu.VMEM((2, 1, g), F32),
            pltpu.VMEM((2, n_frame * n_patch, 1, g), F32),
            pltpu.VMEM((8, g), F32),
            dma((blocks // 2,)),
            dma(()),
            dma((2, 2, 2)),
            dma((2, 2)),
            dma((2, 2)),
            pltpu.SemaphoreType.REGULAR,
        ],
        compiler_params=pltpu.CompilerParams(
            collective_id=0, has_side_effects=True, vmem_limit_bytes=62 * 1024 * 1024
        ),
    )(
        coeffs.reshape(pairs, modes),
        object_field,
        pupil_mask,
        fwd,
        inv,
        observed.reshape(pairs, g, g),
        mode_basis,
    )
    new_coeffs, new_object = pl.pallas_call(
        pass_on,
        out_shape=[
            jax.ShapeDtypeStruct(new_coeffs.shape, F32),
            jax.ShapeDtypeStruct(new_object.shape, F32),
        ],
    )(new_coeffs, new_object)
    return new_coeffs.reshape(coeffs.shape), new_object


def solution(mesh):
    in_specs = (
        P("frame", "patch", None),
        P("frame", "patch", None, None),
        P("patch", "frame", None),
        P(),
        P(),
    )
    out_specs = (P("frame", "patch", None), P("patch", "frame", None))
    run = functools.partial(local, mesh.shape["frame"], mesh.shape["patch"])
    return jax.shard_map(run, mesh=mesh, in_specs=in_specs, out_specs=out_specs, check_vma=False)
```
